32 devices in a mesh: users: 8 (over y, x, core), seq: 4 (over z).
Axes of the slice: x: 2, y: 2, z: 4, core: 2. Of those that a mesh axis runs over, the one named last changes fastest.
Arguments:
- item_table: bfloat16 [65536, 512], P(('users', 'seq')), may hold values from -6 to 6
- item_ids: int32 [8, 1536], P('users', 'seq'), may hold values from 0 to 65535, as said below
- segment_ids: int32 [8, 1536], P('users', 'seq'), may hold values from 0 to 2, never falling along the last dimension, each value on 1 to 768 neighbouring positions
- weight_in: bfloat16 [512, 2048], replicated, may hold values from -0.25 to 0.25
- weight_out: bfloat16 [512, 512], replicated, may hold values from -0.25 to 0.25
- gain_in: float32 [512], replicated, may hold values from 0.5 to 1.5
- gain_mid: float32 [512], replicated, may hold values from 0.5 to 1.5
- cotangent: bfloat16 [8, 1536, 512], P('users', 'seq'), may hold values from -6 to 6
Outputs:
- layer_out: bfloat16 [8, 1536, 512], P('users', 'seq')
- table_grad: float32 [65536, 512], P(('users', 'seq'))
- weight_in_grad: float32 [512, 2048], replicated
- weight_out_grad: float32 [512, 512], replicated
The draws below stay inside these ranges and needn't reach their ends.
Inputs may be any that keep to these rules, and one draw needn't show every extreme that they name: `item_ids`: row r is held by device r // 2048 counted over users then seq. The 384 events of one device name rows of at most 24 events for each holding device, and in every draw each device has exactly 24 events whose rows one device holds.
All inputs are finite; a program needn't handle non-finite values.
Results may differ from the reference program's by a relative error of at most 0.006.
The reference program's roundings to bfloat16 on the way count: a program that leaves them out, or rounds other values in their place, can miss the bound.
Values may be sent and summed in bfloat16 or wider, within the bound.
A program may use at most 128 MiB of HBM per device.

```python
import math
import jax
import jax.numpy as jnp
import numpy as np
from jax import lax

HEADS = 8
HEAD_DIM = 64
D = 512
L_DEV = 384
ROWS_DEV = 2048
USERS = 8
LEN = 1536
ROWS = 65536
CAP = 24


def draw_item_ids(key, part):
    blocks = USERS * LEN // L_DEV
    slots = blocks * CAP

    def one_block(block_key):
        key_perm, key_owner, key_shuffle, key_rows = jax.random.split(block_key, 4)
        ranking = jax.random.permutation(key_perm, slots)
        favoured = jax.random.randint(key_owner, (), 0, blocks)
        owners_of = jnp.arange(slots) // CAP
        scores = jnp.where(owners_of == favoured, ranking - slots, ranking)
        picked = jnp.argsort(scores, stable=True)[:L_DEV]
        owners = (picked // CAP)[jax.random.permutation(key_shuffle, L_DEV)]
        within = jax.random.randint(key_rows, (L_DEV,), 0, ROWS_DEV)
        return (owners * ROWS_DEV + within).astype(jnp.int32)
    return jax.vmap(one_block)(jax.random.split(key, blocks)).reshape(USERS, LEN)


def level_of(key, dims, shards, low, high):
    def one(dim, blocks):
        steps = jax.random.uniform(jax.random.fold_in(jax.random.fold_in(key, 6), dim), (blocks,), jnp.float32, low / len(shards), high / len(shards))
        return jnp.repeat(jnp.exp(steps), dims[dim] // blocks).reshape((-1,) + (1,) * (len(dims) - dim - 1))

    loudness = one(*shards[0])
    for cut in shards[1:]:
        loudness = loudness * one(*cut)
    return loudness


def split_up(amount, total, limit, lean):
    weights = [(1 << 20) // math.isqrt(standing ** lean) + 1 for standing in range(2, amount + 1)]
    surplus, counts = total - limit - (amount - 1), [1] * (amount - 1)
    while surplus > 0:
        free = [i for i in range(amount - 1) if counts[i] < limit]
        mass, remaining = sum([weights[i] for i in free]), surplus
        for i in free:
            extra = min(limit - counts[i], max(1, remaining * weights[i] // mass), surplus)
            counts[i] = counts[i] + extra
            surplus = surplus - extra
    return np.array([limit] + counts)


def uneven_parts(own_key, number_of, total, reach, slope):
    if number_of == 2:
        one = jax.random.randint(own_key, (), max(1, total - reach), min(reach, total - 1) + 1)
        return jnp.stack([one, total - one])
    sizes = jnp.asarray(split_up(number_of, total, reach, slope), jnp.int32)
    twos = (number_of - 1) // 2
    giver, taker = sizes[1:1 + 2 * twos:2], sizes[2:2 + 2 * twos:2]
    room = jnp.minimum(giver - 1, reach - taker)
    passed = jax.random.randint(jax.random.fold_in(own_key, 1), (twos,), 0, 1 << 20) % (room + 1)
    sizes = sizes.at[1:1 + 2 * twos:2].set(giver - passed).at[2:2 + 2 * twos:2].set(taker + passed)
    return sizes[jax.random.permutation(jax.random.fold_in(own_key, 2), number_of)]


def gaussian(own_key, dims, scale, limit, cuts=(), held_as=jnp.bfloat16):
    loudness = level_of(own_key, dims, cuts, -0.22, 0.18) if cuts else 1.0
    entries = jax.random.normal(own_key, dims, jnp.float32) * scale * loudness
    return jnp.minimum(jnp.maximum(entries, -limit), limit).astype(held_as)


def setup_inputs(seed: int = 0) -> dict:
    key_of = jax.random.split(jax.random.key(seed), 9)
    return {
        "item_table": gaussian(key_of[0], (ROWS, D), 1.0, 6.0, ((0, 32),)),
        "item_ids": draw_item_ids(jax.random.fold_in(key_of[8], 71), 0),
        "segment_ids": jax.vmap(lambda own: jnp.searchsorted(jnp.cumsum(uneven_parts(own, 3, LEN, LEN // 2, 0)), jnp.arange(LEN), side="right"))(jax.random.split(key_of[2], USERS)).reshape((USERS, LEN)).astype(jnp.int32),
        "weight_in": gaussian(key_of[3], (D, 4 * D), D ** -0.5, 0.25),
        "weight_out": gaussian(key_of[4], (D, D), D ** -0.5, 0.25),
        "gain_in": jnp.clip(1.0 + 0.1 * jax.random.normal(key_of[5], (D,), jnp.float32), 0.5, 1.5),
        "gain_mid": jnp.clip(1.0 + 0.1 * jax.random.normal(key_of[6], (D,), jnp.float32), 0.5, 1.5),
        "cotangent": gaussian(key_of[7], (USERS, LEN, D), 1.0, 6.0, ((0, 8), (1, 4))),
    }


epsilon = 1e-05

def normalize(values):
    centred = values - lax.optimization_barrier(jnp.mean(values, axis=-1, keepdims=True))
    inverse = lax.rsqrt(lax.optimization_barrier(jnp.mean(centred * centred, axis=-1, keepdims=True)) + epsilon)
    return (centred * inverse, inverse)

def norm_back(grad_hat, normed, inverse):
    return inverse * (grad_hat - lax.optimization_barrier(jnp.mean(grad_hat, axis=-1, keepdims=True)) - normed * lax.optimization_barrier(jnp.mean(grad_hat * normed, axis=-1, keepdims=True)))

def silu_slope(values):
    sigma = jax.nn.sigmoid(values)
    return sigma * (1.0 + values * (1.0 - sigma))

def split_heads(matrix):
    return matrix.reshape(matrix.shape[0], HEADS, HEAD_DIM).transpose(1, 0, 2)

def join_heads(stacked):
    return stacked.transpose(1, 0, 2).reshape(stacked.shape[1], HEADS * HEAD_DIM)

def head_scores(query, keys, visible):
    scores = jnp.dot(query, keys.T, preferred_element_type=jnp.float32) * HEAD_DIM ** (-0.5)
    weights = jnp.where(visible, jax.nn.silu(scores), 0.0).astype(jnp.bfloat16)
    return (scores, weights)

def score_grads(scores, upstream, values, visible):
    dweights = jnp.dot(upstream, values.T, preferred_element_type=jnp.float32)
    return (jnp.where(visible, dweights * silu_slope(scores), 0.0) * HEAD_DIM ** (-0.5)).astype(jnp.bfloat16)

def reference(item_table, item_ids, segment_ids, weight_in, weight_out, gain_in, gain_mid, cotangent):
    width = weight_out.shape[0]

    def one_user(operands):
        user_ids, user_segments, upstream = operands
        length = user_ids.shape[0]
        fetched = item_table[user_ids]
        fetched_f = fetched.astype(jnp.float32)
        normed_in, inverse_in = normalize(fetched_f)
        normed_b = (normed_in * gain_in).astype(jnp.bfloat16)
        hidden_pre = jnp.dot(normed_b, weight_in, preferred_element_type=jnp.float32)
        hidden = jax.nn.silu(hidden_pre)
        gate_part = hidden[:, :width]
        value_b = hidden[:, width:2 * width].astype(jnp.bfloat16)
        query_b = hidden[:, 2 * width:3 * width].astype(jnp.bfloat16)
        key_b = hidden[:, 3 * width:].astype(jnp.bfloat16)
        position = jnp.arange(length, dtype=jnp.int32)
        visible = (position[None, :] <= position[:, None]) & (user_segments[None, :] == user_segments[:, None])

        def forward_head(triple):
            head_query, head_key, head_value = triple
            scores, weights = head_scores(head_query, head_key, visible)
            return jnp.dot(weights, head_value, preferred_element_type=jnp.float32)
        mixed = join_heads(lax.map(forward_head, (split_heads(query_b), split_heads(key_b), split_heads(value_b))))
        normed_mid, inverse_mid = normalize(mixed)
        scaled_mid = normed_mid * gain_mid
        gated = (scaled_mid * gate_part).astype(jnp.bfloat16)
        layer = (fetched_f + jnp.dot(gated, weight_out, preferred_element_type=jnp.float32)).astype(jnp.bfloat16)
        grad_wout = jnp.dot(gated.T, upstream, preferred_element_type=jnp.float32)
        grad_gated = jnp.dot(upstream, weight_out.T, preferred_element_type=jnp.float32)
        grad_gate = grad_gated * scaled_mid
        grad_mixed = norm_back(grad_gated * gate_part * gain_mid, normed_mid, inverse_mid).astype(jnp.bfloat16)

        def backward_head(quad):
            head_query, head_key, head_value, head_up = quad
            scores, weights = head_scores(head_query, head_key, visible)
            dscores = score_grads(scores, head_up, head_value, visible)
            grad_q = jnp.dot(dscores, head_key, preferred_element_type=jnp.float32)
            grad_k = jnp.dot(dscores.T, head_query, preferred_element_type=jnp.float32)
            grad_v = jnp.dot(weights.T, head_up, preferred_element_type=jnp.float32)
            return (grad_q, grad_k, grad_v)
        stacked_q, stacked_k, stacked_v = lax.map(backward_head, (split_heads(query_b), split_heads(key_b), split_heads(value_b), split_heads(grad_mixed)))
        grad_hidden = jnp.concatenate([grad_gate, join_heads(stacked_v), join_heads(stacked_q), join_heads(stacked_k)], axis=1)
        grad_pre = (grad_hidden * silu_slope(hidden_pre)).astype(jnp.bfloat16)
        grad_win = jnp.dot(normed_b.T, grad_pre, preferred_element_type=jnp.float32)
        grad_normed = jnp.dot(grad_pre, weight_in.T, preferred_element_type=jnp.float32)
        grad_rows = norm_back(grad_normed * gain_in, normed_in, inverse_in) + upstream.astype(jnp.float32)
        return (layer, grad_rows, grad_win, grad_wout)
    layer_out, grad_rows, grad_win, grad_wout = lax.map(one_user, (item_ids, segment_ids, cotangent))
    table_grad = jnp.zeros(item_table.shape, jnp.float32).at[item_ids.reshape(-1)].add(grad_rows.reshape(-1, grad_rows.shape[-1]))
    return (layer_out, table_grad, lax.optimization_barrier(jnp.sum(grad_win, axis=0)), lax.optimization_barrier(jnp.sum(grad_wout, axis=0)))
```

```python
import functools

import jax
import jax.numpy as jnp
from jax import lax
from jax.experimental import pallas as pl
from jax.experimental.pallas import tpu as pltpu
from jax.sharding import PartitionSpec as P

HEADS = 8
HEAD_DIM = 64


epsilon = 1e-05


def normalize(values):
    centred = values - jnp.mean(values, axis=-1, keepdims=True)
    inverse = lax.rsqrt(jnp.mean(centred * centred, axis=-1, keepdims=True) + epsilon)
    return (centred * inverse, inverse)


def norm_back(grad_hat, normed, inverse):
    return inverse * (
        grad_hat
        - jnp.mean(grad_hat, axis=-1, keepdims=True)
        - normed * jnp.mean(grad_hat * normed, axis=-1, keepdims=True)
    )


def silu_slope(values):
    sigma = jax.nn.sigmoid(values)
    return sigma * (1.0 + values * (1.0 - sigma))


PAIR = 2 * HEAD_DIM
SCALE = HEAD_DIM ** (-0.5)


def nt(left, right):
    return lax.dot_general(left, right, (((1,), (1,)), ((), ())), preferred_element_type=jnp.float32)


def silu_parts(scores):
    sigma = 0.5 * jnp.tanh(0.5 * scores) + 0.5
    return sigma, scores * sigma


def visible_of(query_seg, key_seg, rows, columns, row_start, triangular, transposed):
    visible = query_seg == key_seg
    if triangular:
        row = lax.broadcasted_iota(jnp.int32, (rows, columns), 0) + row_start
        column = lax.broadcasted_iota(jnp.int32, (rows, columns), 1)
        visible &= (row <= column) if transposed else (column <= row)
    return visible


def chunk_of(count):
    return 128 if count % 128 == 0 else count


def forward_kernel(triangular, has_acc, flag_ref, q_ref, k_ref, v_ref, segq_ref, segk_ref, *rest):
    acc_ref, out_ref = rest if has_acc else (None, rest[0])
    count = q_ref.shape[0]
    step = chunk_of(count)
    if has_acc:
        out_ref[...] = acc_ref[...]

    def work():
        for start in range(0, count, step):
            rows = slice(start, start + step)
            limit = start + step if triangular else count
            visible = visible_of(
                segq_ref[rows, :], segk_ref[:, :limit], step, limit, start, triangular, False
            )
            parts = []
            for head in range(2):
                lanes = slice(head * HEAD_DIM, (head + 1) * HEAD_DIM)
                scores = nt(q_ref[rows, lanes], k_ref[:limit, lanes]) * SCALE
                _, weights = silu_parts(scores)
                weights = jnp.where(visible, weights, 0.0).astype(jnp.bfloat16)
                parts.append(
                    jnp.dot(weights, v_ref[:limit, lanes], preferred_element_type=jnp.float32)
                )
            both = jnp.concatenate(parts, axis=1)
            if has_acc:
                out_ref[rows, :] += both
            else:
                out_ref[rows, :] = both

    if has_acc:
        pl.when(flag_ref[0] != 0)(work)
    else:
        work()


def query_kernel(shifts, flag_ref, q_ref, up_ref, segq_ref, *rest):
    keys, out_ref = rest[:-1], rest[-1]
    count = q_ref.shape[0]
    step = chunk_of(count)
    for shift in range(shifts + 1):
        k_ref, v_ref, segk_ref = keys[3 * shift : 3 * shift + 3]

        def work(shift=shift, k_ref=k_ref, v_ref=v_ref, segk_ref=segk_ref):
            for start in range(0, count, step):
                rows = slice(start, start + step)
                limit = start + step if shift == 0 else count
                visible = visible_of(
                    segq_ref[rows, :], segk_ref[:, :limit], step, limit, start, shift == 0, False
                )
                parts = []
                for head in range(2):
                    lanes = slice(head * HEAD_DIM, (head + 1) * HEAD_DIM)
                    scores = nt(q_ref[rows, lanes], k_ref[:limit, lanes]) * SCALE
                    sigma, weights = silu_parts(scores)
                    slope = sigma + weights * (1.0 - sigma)
                    dweights = nt(up_ref[rows, lanes], v_ref[:limit, lanes])
                    dscores = jnp.where(visible, dweights * slope, 0.0).astype(jnp.bfloat16)
                    parts.append(
                        jnp.dot(dscores, k_ref[:limit, lanes], preferred_element_type=jnp.float32)
                    )
                both = jnp.concatenate(parts, axis=1) * SCALE
                if shift == 0:
                    out_ref[rows, :] = both
                else:
                    out_ref[rows, :] += both

        if shift == 0:
            work()
        else:
            pl.when(flag_ref[shift - 1] != 0)(work)


def key_kernel(shifts, flag_ref, k_ref, v_ref, segk_ref, *rest):
    queries, (dk_ref, dv_ref) = rest[:-2], rest[-2:]
    count = k_ref.shape[0]
    step = chunk_of(count)
    for shift in range(shifts + 1):
        q_ref, up_ref, segq_ref = queries[3 * shift : 3 * shift + 3]

        def work(shift=shift, q_ref=q_ref, up_ref=up_ref, segq_ref=segq_ref):
            for start in range(0, count, step):
                rows = slice(start, start + step)
                first = start if shift == 0 else 0
                visible = segk_ref[rows, :] == segq_ref[:, first:]
                if shift == 0:
                    row = lax.broadcasted_iota(jnp.int32, (step, count - first), 0)
                    column = lax.broadcasted_iota(jnp.int32, (step, count - first), 1)
                    visible &= row <= column
                parts_k, parts_v = [], []
                for head in range(2):
                    lanes = slice(head * HEAD_DIM, (head + 1) * HEAD_DIM)
                    query, up = q_ref[first:, lanes], up_ref[first:, lanes]
                    scores = nt(k_ref[rows, lanes], query) * SCALE
                    sigma, weights = silu_parts(scores)
                    slope = sigma + weights * (1.0 - sigma)
                    dweights = nt(v_ref[rows, lanes], up)
                    dscores = jnp.where(visible, dweights * slope, 0.0).astype(jnp.bfloat16)
                    weights = jnp.where(visible, weights, 0.0).astype(jnp.bfloat16)
                    parts_k.append(jnp.dot(dscores, query, preferred_element_type=jnp.float32))
                    parts_v.append(jnp.dot(weights, up, preferred_element_type=jnp.float32))
                both_k = jnp.concatenate(parts_k, axis=1) * SCALE
                both_v = jnp.concatenate(parts_v, axis=1)
                if shift == 0:
                    dk_ref[rows, :] = both_k
                    dv_ref[rows, :] = both_v
                else:
                    dk_ref[rows, :] += both_k
                    dv_ref[rows, :] += both_v

        if shift == 0:
            work()
        else:
            pl.when(flag_ref[shift - 1] != 0)(work)


def attention_call(kernel, count, width, operands, results, flops):
    specs = []
    for operand in operands:
        if operand.ndim == 1:
            specs.append(pl.BlockSpec(memory_space=pltpu.SMEM))
        elif operand.shape[1] == width and operand.shape[0] == count:
            specs.append(pl.BlockSpec((count, PAIR), lambda i: (0, i)))
        else:
            specs.append(pl.BlockSpec(operand.shape, lambda i: (0, 0)))
    out = pl.BlockSpec((count, PAIR), lambda i: (0, i))
    shape = jax.ShapeDtypeStruct((count, width), jnp.float32)
    return pl.pallas_call(
        kernel,
        grid=(width // PAIR,),
        in_specs=specs,
        out_specs=[out] * results,
        out_shape=[shape] * results,
        cost_estimate=pl.CostEstimate(
            flops=flops, bytes_accessed=count * width * 2 * len(operands), transcendentals=flops // 256
        ),
    )(*operands)


def body(item_table, item_ids, segment_ids, weight_in, weight_out, gain_in, gain_mid, cotangent):
    events = item_ids[0]
    segments = segment_ids[0]
    upstream = cotangent[0]
    ring = lax.axis_size("seq")
    shifts = (ring + 1) // 2
    forward = [(i, i + 1) for i in range(ring - 1)]
    backward = [(i + 1, i) for i in range(ring - 1)]
    marked = segments + 1
    before, after = [marked], [marked]
    for shift in range(1, shifts + 1):
        before.append(lax.ppermute(marked, "seq", [(i, i + shift) for i in range(ring - shift)]))
        after.append(lax.ppermute(marked, "seq", [(i + shift, i) for i in range(ring - shift)]))
    before_flags = jnp.stack([(seg[-1] == marked[0]).astype(jnp.int32) for seg in before[1:]])
    after_flags = jnp.stack([(seg[0] == marked[-1]).astype(jnp.int32) for seg in after[1:]])
    count = events.shape[0]
    shard_rows = item_table.shape[0]
    width = item_table.shape[1]
    devices = lax.axis_size(("users", "seq"))
    capacity = 2 * count // devices
    owner_index = events // shard_rows
    owner_hits = (owner_index[:, None] == jnp.arange(devices, dtype=jnp.int32)[None, :]).astype(
        jnp.int32
    )
    arrival = jnp.sum(jnp.cumsum(owner_hits, axis=0) * owner_hits, axis=1) - 1
    slot_of = owner_index * capacity + arrival
    wanted = jnp.zeros((devices * capacity,), jnp.int32).at[slot_of].set(events % shard_rows)
    asked = lax.all_to_all(
        wanted.reshape(devices, capacity), ("users", "seq"), split_axis=0, concat_axis=0, tiled=True
    )
    asked = asked.reshape(-1)
    served = item_table[asked]
    returned = lax.all_to_all(
        served.reshape(devices, capacity, width),
        ("users", "seq"),
        split_axis=0,
        concat_axis=0,
        tiled=True,
    )
    fetched = returned.reshape(devices * capacity, width)[slot_of]
    fetched_f = fetched.astype(jnp.float32)
    normed_in, inverse_in = normalize(fetched_f)
    normed_b = (normed_in * gain_in).astype(jnp.bfloat16)
    hidden_pre = jnp.dot(normed_b, weight_in, preferred_element_type=jnp.float32)
    hidden = jax.nn.silu(hidden_pre)
    gate_part = hidden[:, :width]
    value_b = hidden[:, width : 2 * width].astype(jnp.bfloat16)
    query_b = hidden[:, 2 * width : 3 * width].astype(jnp.bfloat16)
    key_b = hidden[:, 3 * width :].astype(jnp.bfloat16)
    keys, values = [key_b], [value_b]
    queries = [query_b]
    for shift in range(shifts):
        keys.append(lax.ppermute(keys[-1], "seq", forward))
        values.append(lax.ppermute(values[-1], "seq", forward))
        queries.append(lax.ppermute(queries[-1], "seq", backward))
    unit = 2 * count * count * width
    mixed = None
    for shift in range(shifts + 1):
        operands = [
            before_flags[max(shift - 1, 0)][None],
            query_b,
            keys[shift],
            values[shift],
            marked[:, None],
            before[shift][None, :],
        ]
        if shift:
            operands.append(mixed)
        (mixed,) = attention_call(
            functools.partial(forward_kernel, shift == 0, shift > 0),
            count,
            width,
            operands,
            1,
            2 * unit,
        )
    normed_mid, inverse_mid = normalize(mixed)
    scaled_mid = normed_mid * gain_mid
    gated = (scaled_mid * gate_part).astype(jnp.bfloat16)
    grad_gated = jnp.einsum("te,de->td", upstream, weight_out, preferred_element_type=jnp.float32)
    grad_gate = grad_gated * scaled_mid
    grad_mixed = norm_back(grad_gated * gate_part * gain_mid, normed_mid, inverse_mid).astype(
        jnp.bfloat16
    )
    ups = [grad_mixed]
    for shift in range(shifts):
        ups.append(lax.ppermute(ups[-1], "seq", backward))
    layer = (fetched_f + jnp.dot(gated, weight_out, preferred_element_type=jnp.float32)).astype(
        jnp.bfloat16
    )
    grad_wout = jnp.einsum("td,te->de", gated, upstream, preferred_element_type=jnp.float32)
    operands = [before_flags, query_b, grad_mixed, marked[:, None]]
    for shift in range(shifts + 1):
        operands += [keys[shift], values[shift], before[shift][None, :]]
    (grad_query,) = attention_call(
        functools.partial(query_kernel, shifts), count, width, operands, 1, 3 * (shifts + 1) * unit
    )
    operands = [after_flags, key_b, value_b, marked[:, None]]
    for shift in range(shifts + 1):
        operands += [queries[shift], ups[shift], after[shift][None, :]]
    grad_key, grad_value = attention_call(
        functools.partial(key_kernel, shifts), count, width, operands, 2, 4 * (shifts + 1) * unit
    )
    gate_pre = (grad_gate * silu_slope(hidden_pre[:, :width])).astype(jnp.bfloat16)
    grad_win_gate = jnp.einsum("td,tf->df", normed_b, gate_pre, preferred_element_type=jnp.float32)
    early_win, weight_out_grad = lax.psum((grad_win_gate, grad_wout), ("users", "seq"))
    grad_rest = jnp.concatenate([grad_value, grad_query, grad_key], axis=1)
    rest_pre = (grad_rest * silu_slope(hidden_pre[:, width:])).astype(jnp.bfloat16)
    grad_pre = jnp.concatenate([gate_pre, rest_pre], axis=1)
    grad_win = jnp.einsum("td,tf->df", normed_b, rest_pre, preferred_element_type=jnp.float32)
    grad_normed = jnp.einsum("tf,df->td", grad_pre, weight_in, preferred_element_type=jnp.float32)
    grad_rows = norm_back(grad_normed * gain_in, normed_in, inverse_in) + upstream.astype(
        jnp.float32
    )
    late_win = lax.psum(grad_win, ("users", "seq"))
    weight_in_grad = jnp.concatenate([early_win, late_win], axis=1)
    outgoing = jnp.zeros((devices * capacity, width), jnp.float32).at[slot_of].set(grad_rows)
    incoming = lax.all_to_all(
        outgoing.reshape(devices, capacity, width).astype(jnp.bfloat16),
        ("users", "seq"),
        split_axis=0,
        concat_axis=0,
        tiled=True,
    ).astype(jnp.float32)
    table_grad = (
        jnp.zeros((shard_rows, width), jnp.float32)
        .at[asked]
        .add(incoming.reshape(devices * capacity, width))
    )
    return (layer[None], table_grad, weight_in_grad, weight_out_grad)


def solution(mesh):
    in_specs = (
        P(("users", "seq"), None),
        P("users", "seq"),
        P("users", "seq"),
        P(),
        P(),
        P(),
        P(),
        P("users", "seq", None),
    )
    out_specs = (P("users", "seq", None), P(("users", "seq"), None), P(), P())
    return jax.shard_map(body, mesh=mesh, in_specs=in_specs, out_specs=out_specs, check_vma=False)
```

```python
import functools

import jax
import jax.numpy as jnp
from jax import lax
from jax.experimental import pallas as pl
from jax.experimental.pallas import tpu as pltpu
from jax.sharding import PartitionSpec as P

HEADS = 8
HEAD_DIM = 64


epsilon = 1e-05


def normalize(values):
    centred = values - jnp.mean(values, axis=-1, keepdims=True)
    inverse = lax.rsqrt(jnp.mean(centred * centred, axis=-1, keepdims=True) + epsilon)
    return (centred * inverse, inverse)


def norm_back(grad_hat, normed, inverse):
    return inverse * (
        grad_hat
        - jnp.mean(grad_hat, axis=-1, keepdims=True)
        - normed * jnp.mean(grad_hat * normed, axis=-1, keepdims=True)
    )


def silu_slope(values):
    sigma = jax.nn.sigmoid(values)
    return sigma * (1.0 + values * (1.0 - sigma))


PAIR = 2 * HEAD_DIM
SCALE = HEAD_DIM ** (-0.5)


def nt(left, right):
    return lax.dot_general(left, right, (((1,), (1,)), ((), ())), preferred_element_type=jnp.float32)


def silu_parts(scores):
    sigma = 0.5 * jnp.tanh(0.5 * scores) + 0.5
    return sigma, scores * sigma


def visible_of(query_seg, key_seg, rows, columns, row_start, triangular, transposed):
    visible = query_seg == key_seg
    if triangular:
        row = lax.broadcasted_iota(jnp.int32, (rows, columns), 0) + row_start
        column = lax.broadcasted_iota(jnp.int32, (rows, columns), 1)
        visible &= (row <= column) if transposed else (column <= row)
    return visible


def chunk_of(count):
    return 128 if count % 128 == 0 else count


def forward_kernel(triangular, has_acc, flag_ref, q_ref, k_ref, v_ref, segq_ref, segk_ref, *rest):
    acc_ref, out_ref = rest if has_acc else (None, rest[0])
    count = q_ref.shape[0]
    step = chunk_of(count)
    if has_acc:
        out_ref[...] = acc_ref[...]

    def work():
        for start in range(0, count, step):
            rows = slice(start, start + step)
            limit = start + step if triangular else count
            visible = visible_of(
                segq_ref[rows, :], segk_ref[:, :limit], step, limit, start, triangular, False
            )
            parts = []
            for head in range(2):
                lanes = slice(head * HEAD_DIM, (head + 1) * HEAD_DIM)
                scores = nt(q_ref[rows, lanes], k_ref[:limit, lanes]) * SCALE
                _, weights = silu_parts(scores)
                weights = jnp.where(visible, weights, 0.0).astype(jnp.bfloat16)
                parts.append(
                    jnp.dot(weights, v_ref[:limit, lanes], preferred_element_type=jnp.float32)
                )
            both = jnp.concatenate(parts, axis=1)
            if has_acc:
                out_ref[rows, :] += both
            else:
                out_ref[rows, :] = both

    if has_acc:
        pl.when(flag_ref[0] != 0)(work)
    else:
        work()


def query_kernel(shifts, flag_ref, q_ref, up_ref, segq_ref, *rest):
    keys, out_ref = rest[:-1], rest[-1]
    count = q_ref.shape[0]
    step = chunk_of(count)
    for shift in range(shifts + 1):
        k_ref, v_ref, segk_ref = keys[3 * shift : 3 * shift + 3]

        def work(shift=shift, k_ref=k_ref, v_ref=v_ref, segk_ref=segk_ref):
            for start in range(0, count, step):
                rows = slice(start, start + step)
                limit = start + step if shift == 0 else count
                visible = visible_of(
                    segq_ref[rows, :], segk_ref[:, :limit], step, limit, start, shift == 0, False
                )
                parts = []
                for head in range(2):
                    lanes = slice(head * HEAD_DIM, (head + 1) * HEAD_DIM)
                    scores = nt(q_ref[rows, lanes], k_ref[:limit, lanes]) * SCALE
                    sigma, weights = silu_parts(scores)
                    slope = sigma + weights * (1.0 - sigma)
                    dweights = nt(up_ref[rows, lanes], v_ref[:limit, lanes])
                    dscores = jnp.where(visible, dweights * slope, 0.0).astype(jnp.bfloat16)
                    parts.append(
                        jnp.dot(dscores, k_ref[:limit, lanes], preferred_element_type=jnp.float32)
                    )
                both = jnp.concatenate(parts, axis=1) * SCALE
                if shift == 0:
                    out_ref[rows, :] = both
                else:
                    out_ref[rows, :] += both

        if shift == 0:
            work()
        else:
            pl.when(flag_ref[shift - 1] != 0)(work)


def key_kernel(shifts, flag_ref, k_ref, v_ref, segk_ref, *rest):
    queries, (dk_ref, dv_ref) = rest[:-2], rest[-2:]
    count = k_ref.shape[0]
    step = chunk_of(count)
    for shift in range(shifts + 1):
        q_ref, up_ref, segq_ref = queries[3 * shift : 3 * shift + 3]

        def work(shift=shift, q_ref=q_ref, up_ref=up_ref, segq_ref=segq_ref):
            for start in range(0, count, step):
                rows = slice(start, start + step)
                first = start if shift == 0 else 0
                visible = segk_ref[rows, :] == segq_ref[:, first:]
                if shift == 0:
                    row = lax.broadcasted_iota(jnp.int32, (step, count - first), 0)
                    column = lax.broadcasted_iota(jnp.int32, (step, count - first), 1)
                    visible &= row <= column
                parts_k, parts_v = [], []
                for head in range(2):
                    lanes = slice(head * HEAD_DIM, (head + 1) * HEAD_DIM)
                    query, up = q_ref[first:, lanes], up_ref[first:, lanes]
                    scores = nt(k_ref[rows, lanes], query) * SCALE
                    sigma, weights = silu_parts(scores)
                    slope = sigma + weights * (1.0 - sigma)
                    dweights = nt(v_ref[rows, lanes], up)
                    dscores = jnp.where(visible, dweights * slope, 0.0).astype(jnp.bfloat16)
                    weights = jnp.where(visible, weights, 0.0).astype(jnp.bfloat16)
                    parts_k.append(jnp.dot(dscores, query, preferred_element_type=jnp.float32))
                    parts_v.append(jnp.dot(weights, up, preferred_element_type=jnp.float32))
                both_k = jnp.concatenate(parts_k, axis=1) * SCALE
                both_v = jnp.concatenate(parts_v, axis=1)
                if shift == 0:
                    dk_ref[rows, :] = both_k
                    dv_ref[rows, :] = both_v
                else:
                    dk_ref[rows, :] += both_k
                    dv_ref[rows, :] += both_v

        if shift == 0:
            work()
        else:
            pl.when(flag_ref[shift - 1] != 0)(work)


def attention_call(kernel, count, width, operands, results, flops):
    specs = []
    for operand in operands:
        if operand.ndim == 1:
            specs.append(pl.BlockSpec(memory_space=pltpu.SMEM))
        elif operand.shape[1] == width and operand.shape[0] == count:
            specs.append(pl.BlockSpec((count, PAIR), lambda i: (0, i)))
        else:
            specs.append(pl.BlockSpec(operand.shape, lambda i: (0, 0)))
    out = pl.BlockSpec((count, PAIR), lambda i: (0, i))
    shape = jax.ShapeDtypeStruct((count, width), jnp.float32)
    return pl.pallas_call(
        kernel,
        grid=(width // PAIR,),
        in_specs=specs,
        out_specs=[out] * results,
        out_shape=[shape] * results,
        cost_estimate=pl.CostEstimate(
            flops=flops, bytes_accessed=count * width * 2 * len(operands), transcendentals=flops // 256
        ),
    )(*operands)


MESH_ID = pl.DeviceIdType.MESH
LANES = 128


def place(index, ring):
    return (index // ring, lax.rem(index, ring))


def my_index():
    return lax.axis_index("users") * lax.axis_size("seq") + lax.axis_index("seq")


def greet_all(devices, ring):
    barrier = pltpu.get_barrier_semaphore()
    me = my_index()

    def greet(step, carry):
        target = place(lax.rem(me + step, devices), ring)
        pl.semaphore_signal(barrier, inc=1, device_id=target, device_id_type=MESH_ID)
        return carry

    lax.fori_loop(1, devices, greet, 0)
    pl.semaphore_wait(barrier, devices - 1)


def exchange_copy(devices, ring, step, out_ref, in_ref, send_sem, recv_sem):
    me = my_index()
    target = lax.rem(me + step, devices)
    return pltpu.make_async_remote_copy(
        src_ref=out_ref.at[target],
        dst_ref=in_ref.at[me],
        send_sem=send_sem.at[step],
        recv_sem=recv_sem.at[step],
        device_id=place(target, ring),
        device_id_type=MESH_ID,
    )


def exchange_start(devices, ring, out_ref, in_ref, send_sem, recv_sem):
    me = my_index()

    def start(step, carry):
        exchange_copy(devices, ring, step, out_ref, in_ref, send_sem, recv_sem).start()
        return carry

    lax.fori_loop(1, devices, start, 0)
    pltpu.make_async_copy(out_ref.at[me], in_ref.at[me], send_sem.at[0]).start()


def exchange_wait(devices, ring, out_ref, in_ref, send_sem, recv_sem):
    me = my_index()

    def wait(step, carry):
        exchange_copy(devices, ring, step, out_ref, in_ref, send_sem, recv_sem).wait()
        return carry

    lax.fori_loop(1, devices, wait, 0)
    pltpu.make_async_copy(out_ref.at[me], in_ref.at[me], send_sem.at[0]).wait()


def exchange_kernel(devices, ring, out_ref, in_ref, send_sem, recv_sem):
    greet_all(devices, ring)
    exchange_start(devices, ring, out_ref, in_ref, send_sem, recv_sem)
    exchange_wait(devices, ring, out_ref, in_ref, send_sem, recv_sem)


def exchange(blocks, identity):
    devices, ring = blocks.shape[0], lax.axis_size("seq")
    return pl.pallas_call(
        functools.partial(exchange_kernel, devices, ring),
        out_shape=jax.ShapeDtypeStruct(blocks.shape, blocks.dtype),
        in_specs=[pl.BlockSpec(memory_space=pltpu.VMEM)],
        out_specs=pl.BlockSpec(memory_space=pltpu.VMEM),
        scratch_shapes=[pltpu.SemaphoreType.DMA((devices,)), pltpu.SemaphoreType.DMA((devices,))],
        compiler_params=pltpu.CompilerParams(collective_id=identity, has_side_effects=True),
    )(blocks)


ROWS_UNIT = 16


def bits_of(size):
    return [1 << bit for bit in range(size.bit_length() - 1)]


def orders_of(users, parts):
    bits = bits_of(users)
    turned = bits[:1] + bits[1:][::-1]
    return [bits, turned][:parts]


def chunks(total, start_of, body):
    group = 4 if total % 4 == 0 else total

    def step(index, carry):
        body(index * group, group)
        return carry

    lax.fori_loop(0, total // group, step, 0)


def reduce_kernel(users, ring, parts, pieces, *refs):
    stages = len(bits_of(users))
    win_ref, wout_ref, out_ref, win_out, wout_out, in_ref, acc, gathered = refs[:8]
    rest = list(refs[8:])
    sends = [[rest.pop(0) for _ in range(stages + 1)] for _ in range(parts)]
    recvs = [[rest.pop(0) for _ in range(stages + 1)] for _ in range(parts)]
    a2a_send, a2a_recv, half_send, half_recv, ring_send, ring_recv = rest[:6]
    back_send, back_recv, share_send, share_recv = rest[6:]
    devices = users * ring
    me_u, me_s = lax.axis_index("users"), lax.axis_index("seq")
    units = acc.shape[0]
    span = acc.shape[2]
    win_width = win_ref.shape[1]
    orders = orders_of(users, parts)
    per_part = units // parts

    def packed(block):
        rows = pl.ds(pl.multiple_of(block * ROWS_UNIT, ROWS_UNIT), ROWS_UNIT)
        both = jnp.concatenate([win_ref[rows, :], wout_ref[rows, :]], axis=1)
        return [both[:, piece * span : (piece + 1) * span] for piece in range(pieces)]

    greet_all(devices, ring)
    exchange_start(devices, ring, out_ref, in_ref, a2a_send, a2a_recv)

    def bit_at(order, stage):
        return lax.rem(me_u // order[stage], 2)

    def partner_of(order, stage):
        bit = bit_at(order, stage)
        return (me_u + order[stage] - 2 * order[stage] * bit, me_s)

    bases = [part * per_part for part in range(parts)]
    size = per_part
    history = []
    for stage in range(stages):
        half = size // 2
        history.append((list(bases), half))
        copies = []
        for part in range(parts):
            bit = bit_at(orders[part], stage)
            keep, give = bases[part] + bit * half, bases[part] + (1 - bit) * half
            buffer = sends[part][stage]
            if stage == 0:

                def pack_give(index, carry, give=give, buffer=buffer):
                    for piece, value in enumerate(packed(give // pieces + index)):
                        buffer[index * pieces + piece] = value.astype(jnp.bfloat16)
                    return carry

                lax.fori_loop(0, half // pieces, pack_give, 0)
            else:

                def cast_give(first, group, give=give, buffer=buffer):
                    buffer[pl.ds(first, group)] = acc[pl.ds(give + first, group)].astype(jnp.bfloat16)

                chunks(half, 0, cast_give)
            copy = pltpu.make_async_remote_copy(
                src_ref=buffer,
                dst_ref=recvs[part][stage],
                send_sem=half_send.at[part, stage],
                recv_sem=half_recv.at[part, stage],
                device_id=partner_of(orders[part], stage),
                device_id_type=MESH_ID,
            )
            copy.start()
            copies.append(copy)
            bases[part] = keep
        for part in range(parts):
            keep, buffer = bases[part], recvs[part][stage]
            copies[part].wait()
            if stage == 0:

                def pack_keep(index, carry, keep=keep, buffer=buffer):
                    for piece, value in enumerate(packed(keep // pieces + index)):
                        unit = index * pieces + piece
                        acc[keep + unit] = value + buffer[unit].astype(jnp.float32)
                    return carry

                lax.fori_loop(0, half // pieces, pack_keep, 0)
            else:

                def add_keep(first, group, keep=keep, buffer=buffer):
                    acc[pl.ds(keep + first, group)] += buffer[pl.ds(first, group)].astype(jnp.float32)

                chunks(half, 0, add_keep)
        size = half

    own = size // ring
    copies = []
    for part in range(parts):
        buffer = sends[part][stages]

        def cast_ring(first, group, base=bases[part], buffer=buffer):
            buffer[pl.ds(first, group)] = acc[pl.ds(base + first, group)].astype(jnp.bfloat16)

        chunks(size, 0, cast_ring)
        for step in range(1, ring):
            target = lax.rem(me_s + step, ring)
            copy = pltpu.make_async_remote_copy(
                src_ref=buffer.at[pl.ds(target * own, own)],
                dst_ref=recvs[part][stages].at[step - 1],
                send_sem=ring_send.at[part, step - 1],
                recv_sem=ring_recv.at[part, step - 1],
                device_id=(me_u, target),
                device_id_type=MESH_ID,
            )
            copy.start()
            copies.append(copy)
    for copy in copies:
        copy.wait()
    copies = []
    for part in range(parts):
        mine = bases[part] + me_s * own
        for unit in range(own):
            total = acc[mine + unit]
            for step in range(1, ring):
                total = total + recvs[part][stages][step - 1, unit].astype(jnp.float32)
            gathered[mine + unit] = total.astype(jnp.bfloat16)
        for step in range(1, ring):
            target = lax.rem(me_s + step, ring)
            copy = pltpu.make_async_remote_copy(
                src_ref=gathered.at[pl.ds(mine, own)],
                dst_ref=gathered.at[pl.ds(mine, own)],
                send_sem=share_send.at[part, step - 1],
                recv_sem=share_recv.at[part, step - 1],
                device_id=(me_u, target),
                device_id_type=MESH_ID,
            )
            copy.start()
            copies.append(copy)
    for copy in copies:
        copy.wait()
    for stage in reversed(range(stages)):
        copies = []
        for part in range(parts):
            held = pl.ds(bases[part], size)
            copy = pltpu.make_async_remote_copy(
                src_ref=gathered.at[held],
                dst_ref=gathered.at[held],
                send_sem=back_send.at[part, stage],
                recv_sem=back_recv.at[part, stage],
                device_id=partner_of(orders[part], stage),
                device_id_type=MESH_ID,
            )
            copy.start()
            copies.append(copy)
        for copy in copies:
            copy.wait()
        bases, size = history[stage][0], size * 2

    def unpack(block, carry):
        rows = pl.ds(pl.multiple_of(block * ROWS_UNIT, ROWS_UNIT), ROWS_UNIT)
        both = jnp.concatenate(
            [gathered[block * pieces + piece].astype(jnp.float32) for piece in range(pieces)], axis=1
        )
        win_out[rows, :] = both[:, :win_width]
        wout_out[rows, :] = both[:, win_width:]
        return carry

    lax.fori_loop(0, units // pieces, unpack, 0)
    exchange_wait(devices, ring, out_ref, in_ref, a2a_send, a2a_recv)


def reduce_and_exchange(grad_win, grad_wout, outgoing, identity):
    users, ring = lax.axis_size("users"), lax.axis_size("seq")
    devices = users * ring
    rows, width = grad_win.shape[0], grad_win.shape[1] + grad_wout.shape[1]
    pieces = 4
    span = width // pieces
    units = rows // ROWS_UNIT * pieces
    parts = 2 if units // 2 % devices == 0 else 1
    stages = len(bits_of(users))
    sizes = [units // parts >> (stage + 1) for stage in range(stages)]
    unit = (ROWS_UNIT, span)
    last = sizes[-1]
    send = [pltpu.VMEM((size, *unit), jnp.bfloat16) for size in sizes + [last]]
    recv = [pltpu.VMEM((size, *unit), jnp.bfloat16) for size in sizes]
    recv.append(pltpu.VMEM((ring - 1, last // ring, *unit), jnp.bfloat16))
    dma = pltpu.SemaphoreType.DMA
    vmem = pl.BlockSpec(memory_space=pltpu.VMEM)
    return pl.pallas_call(
        functools.partial(reduce_kernel, users, ring, parts, pieces),
        out_shape=[
            jax.ShapeDtypeStruct(grad_win.shape, jnp.float32),
            jax.ShapeDtypeStruct(grad_wout.shape, jnp.float32),
            jax.ShapeDtypeStruct(outgoing.shape, outgoing.dtype),
        ],
        in_specs=[vmem] * 3,
        out_specs=[vmem] * 3,
        scratch_shapes=[
            pltpu.VMEM((units, *unit), jnp.float32),
            pltpu.VMEM((units, *unit), jnp.bfloat16),
            *(send * parts),
            *(recv * parts),
            dma((devices,)),
            dma((devices,)),
            dma((parts, stages)),
            dma((parts, stages)),
            dma((parts, ring - 1)),
            dma((parts, ring - 1)),
            dma((parts, stages)),
            dma((parts, stages)),
            dma((parts, ring - 1)),
            dma((parts, ring - 1)),
        ],
        compiler_params=pltpu.CompilerParams(
            collective_id=identity, has_side_effects=True, vmem_limit_bytes=48 * 1024 * 1024
        ),
    )(grad_win, grad_wout, outgoing)


def row_at(table, index):
    return lax.dynamic_slice_in_dim(table, index, 1)[0]


def body(item_table, item_ids, segment_ids, weight_in, weight_out, gain_in, gain_mid, cotangent):
    events = item_ids[0]
    segments = segment_ids[0]
    upstream = cotangent[0]
    ring = lax.axis_size("seq")
    shifts = (ring + 1) // 2
    forward = [(i, i + 1) for i in range(ring - 1)]
    backward = [(i + 1, i) for i in range(ring - 1)]
    marked = segments + 1
    count = events.shape[0]
    shard_rows = item_table.shape[0]
    width = item_table.shape[1]
    devices = lax.axis_size(("users", "seq"))
    capacity = 2 * count // devices
    owner_index = events // shard_rows
    owner_hits = (owner_index[:, None] == jnp.arange(devices, dtype=jnp.int32)[None, :]).astype(
        jnp.int32
    )
    arrival = jnp.sum(jnp.cumsum(owner_hits, axis=0) * owner_hits, axis=1) - 1
    slot_of = owner_index * capacity + arrival
    wanted = jnp.zeros((devices * capacity,), jnp.int32).at[slot_of].set(events % shard_rows)
    requests = jnp.pad(wanted.reshape(devices, 1, capacity), ((0, 0), (0, 0), (0, LANES - capacity)))
    known = jnp.broadcast_to(marked.reshape(1, count // LANES, LANES), (devices, count // LANES, LANES))
    told = exchange(jnp.concatenate([requests, known], axis=1), 1)
    asked = told[:, 0, :capacity].reshape(-1)
    here = lax.axis_index("seq")
    row = lax.dynamic_slice_in_dim(told[:, 1:], lax.axis_index("users") * ring, ring)
    row = jnp.pad(row.reshape(ring, count), ((shifts, shifts), (0, 0)))
    before = [row_at(row, here + shifts - shift) for shift in range(shifts + 1)]
    after = [row_at(row, here + shifts + shift) for shift in range(shifts + 1)]
    before_flags = jnp.stack([(seg[-1] == marked[0]).astype(jnp.int32) for seg in before[1:]])
    after_flags = jnp.stack([(seg[0] == marked[-1]).astype(jnp.int32) for seg in after[1:]])
    served = item_table[asked]
    returned = exchange(served.reshape(devices, capacity, width), 2)
    fetched = returned.reshape(devices * capacity, width)[slot_of]
    fetched_f = fetched.astype(jnp.float32)
    normed_in, inverse_in = normalize(fetched_f)
    normed_b = (normed_in * gain_in).astype(jnp.bfloat16)
    hidden_pre = jnp.dot(normed_b, weight_in, preferred_element_type=jnp.float32)
    hidden = jax.nn.silu(hidden_pre)
    gate_part = hidden[:, :width]
    value_b = hidden[:, width : 2 * width].astype(jnp.bfloat16)
    query_b = hidden[:, 2 * width : 3 * width].astype(jnp.bfloat16)
    key_b = hidden[:, 3 * width :].astype(jnp.bfloat16)
    keys, values = [key_b], [value_b]
    queries = [query_b]
    for shift in range(shifts):
        keys.append(lax.ppermute(keys[-1], "seq", forward))
        values.append(lax.ppermute(values[-1], "seq", forward))
        queries.append(lax.ppermute(queries[-1], "seq", backward))
    unit = 2 * count * count * width
    mixed = None
    for shift in range(shifts + 1):
        operands = [
            before_flags[max(shift - 1, 0)][None],
            query_b,
            keys[shift],
            values[shift],
            marked[:, None],
            before[shift][None, :],
        ]
        if shift:
            operands.append(mixed)
        (mixed,) = attention_call(
            functools.partial(forward_kernel, shift == 0, shift > 0),
            count,
            width,
            operands,
            1,
            2 * unit,
        )
    normed_mid, inverse_mid = normalize(mixed)
    scaled_mid = normed_mid * gain_mid
    gated = (scaled_mid * gate_part).astype(jnp.bfloat16)
    grad_gated = jnp.einsum("te,de->td", upstream, weight_out, preferred_element_type=jnp.float32)
    grad_gate = grad_gated * scaled_mid
    grad_mixed = norm_back(grad_gated * gate_part * gain_mid, normed_mid, inverse_mid).astype(
        jnp.bfloat16
    )
    ups = [grad_mixed]
    for shift in range(shifts):
        ups.append(lax.ppermute(ups[-1], "seq", backward))
    layer = (fetched_f + jnp.dot(gated, weight_out, preferred_element_type=jnp.float32)).astype(
        jnp.bfloat16
    )
    grad_wout = jnp.einsum("td,te->de", gated, upstream, preferred_element_type=jnp.float32)
    operands = [before_flags, query_b, grad_mixed, marked[:, None]]
    for shift in range(shifts + 1):
        operands += [keys[shift], values[shift], before[shift][None, :]]
    (grad_query,) = attention_call(
        functools.partial(query_kernel, shifts), count, width, operands, 1, 3 * (shifts + 1) * unit
    )
    operands = [after_flags, key_b, value_b, marked[:, None]]
    for shift in range(shifts + 1):
        operands += [queries[shift], ups[shift], after[shift][None, :]]
    grad_key, grad_value = attention_call(
        functools.partial(key_kernel, shifts), count, width, operands, 2, 4 * (shifts + 1) * unit
    )
    gate_pre = (grad_gate * silu_slope(hidden_pre[:, :width])).astype(jnp.bfloat16)
    grad_rest = jnp.concatenate([grad_value, grad_query, grad_key], axis=1)
    rest_pre = (grad_rest * silu_slope(hidden_pre[:, width:])).astype(jnp.bfloat16)
    grad_pre = jnp.concatenate([gate_pre, rest_pre], axis=1)
    grad_win = jnp.einsum("td,tf->df", normed_b, grad_pre, preferred_element_type=jnp.float32)
    grad_normed = jnp.einsum("tf,df->td", grad_pre, weight_in, preferred_element_type=jnp.float32)
    grad_rows = norm_back(grad_normed * gain_in, normed_in, inverse_in) + upstream.astype(
        jnp.float32
    )
    outgoing = jnp.zeros((devices * capacity, width), jnp.float32).at[slot_of].set(grad_rows)
    weight_in_grad, weight_out_grad, incoming = reduce_and_exchange(
        grad_win, grad_wout, outgoing.reshape(devices, capacity, width).astype(jnp.bfloat16), 3
    )
    incoming = incoming.astype(jnp.float32)
    table_grad = (
        jnp.zeros((shard_rows, width), jnp.float32)
        .at[asked]
        .add(incoming.reshape(devices * capacity, width))
    )
    return (layer[None], table_grad, weight_in_grad, weight_out_grad)


def solution(mesh):
    in_specs = (
        P(("users", "seq"), None),
        P("users", "seq"),
        P("users", "seq"),
        P(),
        P(),
        P(),
        P(),
        P("users", "seq", None),
    )
    out_specs = (P("users", "seq", None), P(("users", "seq"), None), P(), P())
    return jax.shard_map(body, mesh=mesh, in_specs=in_specs, out_specs=out_specs, check_vma=False)
```

```python
import functools

import jax
import jax.numpy as jnp
from jax import lax
from jax.experimental import pallas as pl
from jax.experimental.pallas import tpu as pltpu
from jax.sharding import PartitionSpec as P

HEADS = 8
HEAD_DIM = 64


epsilon = 1e-05


def normalize(values):
    centred = values - jnp.mean(values, axis=-1, keepdims=True)
    inverse = lax.rsqrt(jnp.mean(centred * centred, axis=-1, keepdims=True) + epsilon)
    return (centred * inverse, inverse)


def norm_back(grad_hat, normed, inverse):
    return inverse * (
        grad_hat
        - jnp.mean(grad_hat, axis=-1, keepdims=True)
        - normed * jnp.mean(grad_hat * normed, axis=-1, keepdims=True)
    )


def silu_slope(values):
    sigma = jax.nn.sigmoid(values)
    return sigma * (1.0 + values * (1.0 - sigma))


PAIR = 2 * HEAD_DIM
SCALE = HEAD_DIM ** (-0.5)


def nt(left, right):
    return lax.dot_general(left, right, (((1,), (1,)), ((), ())), preferred_element_type=jnp.float32)


def silu_parts(scores):
    sigma = 0.5 * jnp.tanh(0.5 * scores) + 0.5
    return sigma, scores * sigma


def visible_of(query_seg, key_seg, rows, columns, row_start, triangular, transposed):
    visible = query_seg == key_seg
    if triangular:
        row = lax.broadcasted_iota(jnp.int32, (rows, columns), 0) + row_start
        column = lax.broadcasted_iota(jnp.int32, (rows, columns), 1)
        visible &= (row <= column) if transposed else (column <= row)
    return visible


def chunk_of(count):
    return 128 if count % 128 == 0 else count


def forward_kernel(triangular, has_acc, flag_ref, q_ref, k_ref, v_ref, segq_ref, segk_ref, *rest):
    acc_ref, out_ref = rest if has_acc else (None, rest[0])
    count = q_ref.shape[0]
    step = chunk_of(count)
    if has_acc:
        out_ref[...] = acc_ref[...]

    def work():
        for start in range(0, count, step):
            rows = slice(start, start + step)
            limit = start + step if triangular else count
            visible = visible_of(
                segq_ref[rows, :], segk_ref[:, :limit], step, limit, start, triangular, False
            )
            parts = []
            for head in range(2):
                lanes = slice(head * HEAD_DIM, (head + 1) * HEAD_DIM)
                scores = nt(q_ref[rows, lanes], k_ref[:limit, lanes]) * SCALE
                _, weights = silu_parts(scores)
                weights = jnp.where(visible, weights, 0.0).astype(jnp.bfloat16)
                parts.append(
                    jnp.dot(weights, v_ref[:limit, lanes], preferred_element_type=jnp.float32)
                )
            both = jnp.concatenate(parts, axis=1)
            if has_acc:
                out_ref[rows, :] += both
            else:
                out_ref[rows, :] = both

    if has_acc:
        pl.when(flag_ref[0] != 0)(work)
    else:
        work()


def query_kernel(shifts, flag_ref, q_ref, up_ref, segq_ref, *rest):
    keys, out_ref = rest[:-1], rest[-1]
    count = q_ref.shape[0]
    step = chunk_of(count)
    for shift in range(shifts + 1):
        k_ref, v_ref, segk_ref = keys[3 * shift : 3 * shift + 3]

        def work(shift=shift, k_ref=k_ref, v_ref=v_ref, segk_ref=segk_ref):
            for start in range(0, count, step):
                rows = slice(start, start + step)
                limit = start + step if shift == 0 else count
                visible = visible_of(
                    segq_ref[rows, :], segk_ref[:, :limit], step, limit, start, shift == 0, False
                )
                parts = []
                for head in range(2):
                    lanes = slice(head * HEAD_DIM, (head + 1) * HEAD_DIM)
                    scores = nt(q_ref[rows, lanes], k_ref[:limit, lanes]) * SCALE
                    sigma, weights = silu_parts(scores)
                    slope = sigma + weights * (1.0 - sigma)
                    dweights = nt(up_ref[rows, lanes], v_ref[:limit, lanes])
                    dscores = jnp.where(visible, dweights * slope, 0.0).astype(jnp.bfloat16)
                    parts.append(
                        jnp.dot(dscores, k_ref[:limit, lanes], preferred_element_type=jnp.float32)
                    )
                both = jnp.concatenate(parts, axis=1) * SCALE
                if shift == 0:
                    out_ref[rows, :] = both
                else:
                    out_ref[rows, :] += both

        if shift == 0:
            work()
        else:
            pl.when(flag_ref[shift - 1] != 0)(work)


def key_kernel(triangular, flag_ref, k_ref, v_ref, segk_ref, q_ref, up_ref, segq_ref, *rest):
    dk_ref, dv_ref = rest[-2:]
    count = k_ref.shape[0]
    step = chunk_of(count)
    if not triangular:
        dk_ref[...] = rest[0][...]
        dv_ref[...] = rest[1][...]

    def work():
        for start in range(0, count, step):
            rows = slice(start, start + step)
            first = start if triangular else 0
            visible = segk_ref[rows, :] == segq_ref[:, first:]
            if triangular:
                row = lax.broadcasted_iota(jnp.int32, (step, count - first), 0)
                column = lax.broadcasted_iota(jnp.int32, (step, count - first), 1)
                visible &= row <= column
            parts_k, parts_v = [], []
            for head in range(2):
                lanes = slice(head * HEAD_DIM, (head + 1) * HEAD_DIM)
                query, up = q_ref[first:, lanes], up_ref[first:, lanes]
                scores = nt(k_ref[rows, lanes], query) * SCALE
                sigma, weights = silu_parts(scores)
                slope = sigma + weights * (1.0 - sigma)
                dweights = nt(v_ref[rows, lanes], up)
                dscores = jnp.where(visible, dweights * slope, 0.0).astype(jnp.bfloat16)
                weights = jnp.where(visible, weights, 0.0).astype(jnp.bfloat16)
                parts_k.append(jnp.dot(dscores, query, preferred_element_type=jnp.float32))
                parts_v.append(jnp.dot(weights, up, preferred_element_type=jnp.float32))
            both_k = jnp.concatenate(parts_k, axis=1) * SCALE
            both_v = jnp.concatenate(parts_v, axis=1)
            if triangular:
                dk_ref[rows, :] = both_k
                dv_ref[rows, :] = both_v
            else:
                dk_ref[rows, :] += both_k
                dv_ref[rows, :] += both_v

    if triangular:
        work()
    else:
        pl.when(flag_ref[0] != 0)(work)


def attention_call(kernel, count, width, operands, results, micros):
    shift_of = lambda offset: (lambda i: (0, i + offset))
    specs, arrays = [], []
    for operand in operands:
        array, offset = operand if isinstance(operand, tuple) else (operand, 0)
        arrays.append(array)
        if array.ndim == 1:
            specs.append(pl.BlockSpec(memory_space=pltpu.SMEM))
        elif array.shape[0] == count and array.shape[1] % width == 0:
            specs.append(pl.BlockSpec((count, PAIR), shift_of(offset * (width // PAIR))))
        else:
            specs.append(pl.BlockSpec(array.shape, lambda i: (0, 0)))
    out = pl.BlockSpec((count, PAIR), lambda i: (0, i))
    shape = jax.ShapeDtypeStruct((count, width), jnp.float32)
    return pl.pallas_call(
        kernel,
        grid=(width // PAIR,),
        in_specs=specs,
        out_specs=[out] * results,
        out_shape=[shape] * results,
        cost_estimate=pl.CostEstimate(
            flops=int(micros * 1.1e9), bytes_accessed=count * width * 2, transcendentals=0
        ),
    )(*arrays)


MESH_ID = pl.DeviceIdType.MESH
LANES = 128


def place(index, ring):
    return (index // ring, lax.rem(index, ring))


def my_index():
    return lax.axis_index("users") * lax.axis_size("seq") + lax.axis_index("seq")


def greet_all(devices, ring):
    barrier = pltpu.get_barrier_semaphore()
    me = my_index()

    def greet(step, carry):
        target = place(lax.rem(me + step, devices), ring)
        pl.semaphore_signal(barrier, inc=1, device_id=target, device_id_type=MESH_ID)
        return carry

    lax.fori_loop(1, devices, greet, 0)
    pl.semaphore_wait(barrier, devices - 1)


def exchange_copy(devices, ring, step, out_ref, in_ref, send_sem, recv_sem):
    me = my_index()
    target = lax.rem(me + step, devices)
    return pltpu.make_async_remote_copy(
        src_ref=out_ref.at[target],
        dst_ref=in_ref.at[me],
        send_sem=send_sem.at[step],
        recv_sem=recv_sem.at[step],
        device_id=place(target, ring),
        device_id_type=MESH_ID,
    )


def exchange_start(devices, ring, out_ref, in_ref, send_sem, recv_sem):
    me = my_index()

    def start(step, carry):
        exchange_copy(devices, ring, step, out_ref, in_ref, send_sem, recv_sem).start()
        return carry

    lax.fori_loop(1, devices, start, 0)
    pltpu.make_async_copy(out_ref.at[me], in_ref.at[me], send_sem.at[0]).start()


def exchange_wait(devices, ring, out_ref, in_ref, send_sem, recv_sem):
    me = my_index()

    def wait(step, carry):
        exchange_copy(devices, ring, step, out_ref, in_ref, send_sem, recv_sem).wait()
        return carry

    lax.fori_loop(1, devices, wait, 0)
    pltpu.make_async_copy(out_ref.at[me], in_ref.at[me], send_sem.at[0]).wait()


def exchange_kernel(devices, ring, out_ref, in_ref, send_sem, recv_sem):
    greet_all(devices, ring)
    exchange_start(devices, ring, out_ref, in_ref, send_sem, recv_sem)
    exchange_wait(devices, ring, out_ref, in_ref, send_sem, recv_sem)


def exchange(blocks, identity):
    devices, ring = blocks.shape[0], lax.axis_size("seq")
    return pl.pallas_call(
        functools.partial(exchange_kernel, devices, ring),
        out_shape=jax.ShapeDtypeStruct(blocks.shape, blocks.dtype),
        in_specs=[pl.BlockSpec(memory_space=pltpu.VMEM)],
        out_specs=pl.BlockSpec(memory_space=pltpu.VMEM),
        scratch_shapes=[pltpu.SemaphoreType.DMA((devices,)), pltpu.SemaphoreType.DMA((devices,))],
        compiler_params=pltpu.CompilerParams(collective_id=identity, has_side_effects=True),
    )(blocks)


ROWS_UNIT = 16


def bits_of(size):
    return [1 << bit for bit in range(size.bit_length() - 1)]


def orders_of(users, parts):
    bits = bits_of(users)
    turned = bits[:1] + bits[1:][::-1]
    return [bits, turned][:parts]


def chunks(total, start_of, body):
    group = 4 if total % 4 == 0 else total

    def step(index, carry):
        body(index * group, group)
        return carry

    lax.fori_loop(0, total // group, step, 0)


def reduce_kernel(users, ring, parts, pieces, *refs):
    stages = len(bits_of(users))
    win_ref, wout_ref, out_ref, win_out, wout_out, in_ref, acc, gathered = refs[:8]
    rest = list(refs[8:])
    sends = [[rest.pop(0) for _ in range(stages + 1)] for _ in range(parts)]
    recvs = [[rest.pop(0) for _ in range(stages + 1)] for _ in range(parts)]
    a2a_send, a2a_recv, half_send, half_recv, ring_send, ring_recv = rest[:6]
    back_send, back_recv, share_send, share_recv = rest[6:]
    devices = users * ring
    me_u, me_s = lax.axis_index("users"), lax.axis_index("seq")
    units = acc.shape[0]
    span = acc.shape[2]
    win_width = win_ref.shape[1]
    orders = orders_of(users, parts)
    per_part = units // parts

    def packed(block):
        rows = pl.ds(pl.multiple_of(block * ROWS_UNIT, ROWS_UNIT), ROWS_UNIT)
        both = jnp.concatenate([win_ref[rows, :], wout_ref[rows, :]], axis=1)
        return [both[:, piece * span : (piece + 1) * span] for piece in range(pieces)]

    greet_all(devices, ring)
    exchange_start(devices, ring, out_ref, in_ref, a2a_send, a2a_recv)

    def bit_at(order, stage):
        return lax.rem(me_u // order[stage], 2)

    def partner_of(order, stage):
        bit = bit_at(order, stage)
        return (me_u + order[stage] - 2 * order[stage] * bit, me_s)

    bases = [part * per_part for part in range(parts)]
    size = per_part
    history = []
    for stage in range(stages):
        half = size // 2
        history.append((list(bases), half))
        copies = []
        for part in range(parts):
            bit = bit_at(orders[part], stage)
            keep, give = bases[part] + bit * half, bases[part] + (1 - bit) * half
            buffer = sends[part][stage]
            if stage == 0:

                def pack_give(index, carry, give=give, buffer=buffer):
                    for piece, value in enumerate(packed(give // pieces + index)):
                        buffer[index * pieces + piece] = value.astype(jnp.bfloat16)
                    return carry

                lax.fori_loop(0, half // pieces, pack_give, 0)
            else:

                def cast_give(first, group, give=give, buffer=buffer):
                    buffer[pl.ds(first, group)] = acc[pl.ds(give + first, group)].astype(jnp.bfloat16)

                chunks(half, 0, cast_give)
            copy = pltpu.make_async_remote_copy(
                src_ref=buffer,
                dst_ref=recvs[part][stage],
                send_sem=half_send.at[part, stage],
                recv_sem=half_recv.at[part, stage],
                device_id=partner_of(orders[part], stage),
                device_id_type=MESH_ID,
            )
            copy.start()
            copies.append(copy)
            bases[part] = keep
        for part in range(parts):
            keep, buffer = bases[part], recvs[part][stage]
            copies[part].wait()
            if stage == 0:

                def pack_keep(index, carry, keep=keep, buffer=buffer):
                    for piece, value in enumerate(packed(keep // pieces + index)):
                        unit = index * pieces + piece
                        acc[keep + unit] = value + buffer[unit].astype(jnp.float32)
                    return carry

                lax.fori_loop(0, half // pieces, pack_keep, 0)
            else:

                def add_keep(first, group, keep=keep, buffer=buffer):
                    acc[pl.ds(keep + first, group)] += buffer[pl.ds(first, group)].astype(jnp.float32)

                chunks(half, 0, add_keep)
        size = half

    own = size // ring
    copies = []
    for part in range(parts):
        buffer = sends[part][stages]

        def cast_ring(first, group, base=bases[part], buffer=buffer):
            buffer[pl.ds(first, group)] = acc[pl.ds(base + first, group)].astype(jnp.bfloat16)

        chunks(size, 0, cast_ring)
        for step in range(1, ring):
            target = lax.rem(me_s + step, ring)
            copy = pltpu.make_async_remote_copy(
                src_ref=buffer.at[pl.ds(target * own, own)],
                dst_ref=recvs[part][stages].at[step - 1],
                send_sem=ring_send.at[part, step - 1],
                recv_sem=ring_recv.at[part, step - 1],
                device_id=(me_u, target),
                device_id_type=MESH_ID,
            )
            copy.start()
            copies.append(copy)
    for copy in copies:
        copy.wait()
    copies = []
    for part in range(parts):
        mine = bases[part] + me_s * own
        for unit in range(own):
            total = acc[mine + unit]
            for step in range(1, ring):
                total = total + recvs[part][stages][step - 1, unit].astype(jnp.float32)
            gathered[mine + unit] = total.astype(jnp.bfloat16)
        for step in range(1, ring):
            target = lax.rem(me_s + step, ring)
            copy = pltpu.make_async_remote_copy(
                src_ref=gathered.at[pl.ds(mine, own)],
                dst_ref=gathered.at[pl.ds(mine, own)],
                send_sem=share_send.at[part, step - 1],
                recv_sem=share_recv.at[part, step - 1],
                device_id=(me_u, target),
                device_id_type=MESH_ID,
            )
            copy.start()
            copies.append(copy)
    for copy in copies:
        copy.wait()
    for stage in reversed(range(stages)):
        copies = []
        for part in range(parts):
            held = pl.ds(bases[part], size)
            copy = pltpu.make_async_remote_copy(
                src_ref=gathered.at[held],
                dst_ref=gathered.at[held],
                send_sem=back_send.at[part, stage],
                recv_sem=back_recv.at[part, stage],
                device_id=partner_of(orders[part], stage),
                device_id_type=MESH_ID,
            )
            copy.start()
            copies.append(copy)
        for copy in copies:
            copy.wait()
        bases, size = history[stage][0], size * 2

    def unpack(block, carry):
        rows = pl.ds(pl.multiple_of(block * ROWS_UNIT, ROWS_UNIT), ROWS_UNIT)
        both = jnp.concatenate([gathered[block * pieces + piece] for piece in range(pieces)], axis=1)
        win_out[rows, :] = both[:, :win_width]
        wout_out[rows, :] = both[:, win_width:]
        return carry

    lax.fori_loop(0, units // pieces, unpack, 0)
    exchange_wait(devices, ring, out_ref, in_ref, a2a_send, a2a_recv)


def reduce_and_exchange(grad_win, grad_wout, outgoing, identity):
    users, ring = lax.axis_size("users"), lax.axis_size("seq")
    devices = users * ring
    rows, width = grad_win.shape[0], grad_win.shape[1] + grad_wout.shape[1]
    pieces = 4
    span = width // pieces
    units = rows // ROWS_UNIT * pieces
    parts = 2 if units // 2 % devices == 0 else 1
    stages = len(bits_of(users))
    sizes = [units // parts >> (stage + 1) for stage in range(stages)]
    unit = (ROWS_UNIT, span)
    last = sizes[-1]
    send = [pltpu.VMEM((size, *unit), jnp.bfloat16) for size in sizes + [last]]
    recv = [pltpu.VMEM((size, *unit), jnp.bfloat16) for size in sizes]
    recv.append(pltpu.VMEM((ring - 1, last // ring, *unit), jnp.bfloat16))
    dma = pltpu.SemaphoreType.DMA
    vmem = pl.BlockSpec(memory_space=pltpu.VMEM)
    summed_win, summed_wout, incoming = pl.pallas_call(
        functools.partial(reduce_kernel, users, ring, parts, pieces),
        out_shape=[
            jax.ShapeDtypeStruct(grad_win.shape, jnp.bfloat16),
            jax.ShapeDtypeStruct(grad_wout.shape, jnp.bfloat16),
            jax.ShapeDtypeStruct(outgoing.shape, outgoing.dtype),
        ],
        in_specs=[vmem] * 3,
        out_specs=[vmem] * 3,
        scratch_shapes=[
            pltpu.VMEM((units, *unit), jnp.float32),
            pltpu.VMEM((units, *unit), jnp.bfloat16),
            *(send * parts),
            *(recv * parts),
            dma((devices,)),
            dma((devices,)),
            dma((parts, stages)),
            dma((parts, stages)),
            dma((parts, ring - 1)),
            dma((parts, ring - 1)),
            dma((parts, stages)),
            dma((parts, stages)),
            dma((parts, ring - 1)),
            dma((parts, ring - 1)),
        ],
        compiler_params=pltpu.CompilerParams(
            collective_id=identity, has_side_effects=True, vmem_limit_bytes=48 * 1024 * 1024
        ),
    )(grad_win, grad_wout, outgoing)
    return summed_win.astype(jnp.float32), summed_wout.astype(jnp.float32), incoming


def row_at(table, index):
    return lax.dynamic_slice_in_dim(table, index, 1)[0]


def body(item_table, item_ids, segment_ids, weight_in, weight_out, gain_in, gain_mid, cotangent):
    events = item_ids[0]
    segments = segment_ids[0]
    upstream = cotangent[0]
    ring = lax.axis_size("seq")
    shifts = (ring + 1) // 2
    forward = [(i, i + 1) for i in range(ring - 1)]
    backward = [(i + 1, i) for i in range(ring - 1)]
    marked = segments + 1
    count = events.shape[0]
    shard_rows = item_table.shape[0]
    width = item_table.shape[1]
    devices = lax.axis_size(("users", "seq"))
    capacity = 2 * count // devices
    owner_index = events // shard_rows
    owner_hits = (owner_index[:, None] == jnp.arange(devices, dtype=jnp.int32)[None, :]).astype(
        jnp.int32
    )
    arrival = jnp.sum(jnp.cumsum(owner_hits, axis=0) * owner_hits, axis=1) - 1
    slot_of = owner_index * capacity + arrival
    slots = jnp.arange(devices * capacity, dtype=jnp.int32)
    in_slot = slots[:, None] == slot_of[None, :]
    wanted = jnp.sum(jnp.where(in_slot, (events % shard_rows)[None, :], 0), axis=1)
    in_slot = in_slot.astype(jnp.bfloat16)
    requests = jnp.pad(wanted.reshape(devices, 1, capacity), ((0, 0), (0, 0), (0, LANES - capacity)))
    known = jnp.broadcast_to(marked.reshape(1, count // LANES, LANES), (devices, count // LANES, LANES))
    told = exchange(jnp.concatenate([requests, known], axis=1), 1)
    asked = told[:, 0, :capacity].reshape(-1)
    here = lax.axis_index("seq")
    row = lax.dynamic_slice_in_dim(told[:, 1:], lax.axis_index("users") * ring, ring)
    row = jnp.pad(row.reshape(ring, count), ((shifts, shifts), (0, 0)))
    before = [row_at(row, here + shifts - shift) for shift in range(shifts + 1)]
    after = [row_at(row, here + shifts + shift) for shift in range(shifts + 1)]
    before_flags = jnp.stack([(seg[-1] == marked[0]).astype(jnp.int32) for seg in before[1:]])
    after_flags = jnp.stack([(seg[0] == marked[-1]).astype(jnp.int32) for seg in after[1:]])
    shard = jnp.arange(shard_rows, dtype=jnp.int32)
    served = jnp.dot(
        (asked[:, None] == shard[None, :]).astype(jnp.bfloat16),
        item_table,
        preferred_element_type=jnp.float32,
    ).astype(jnp.bfloat16)
    returned = lax.all_to_all(
        served.reshape(devices, capacity, width),
        ("users", "seq"),
        split_axis=0,
        concat_axis=0,
        tiled=True,
    )
    fetched_f = jnp.dot(
        (slot_of[:, None] == slots[None, :]).astype(jnp.bfloat16),
        returned.reshape(devices * capacity, width),
        preferred_element_type=jnp.float32,
    )
    normed_in, inverse_in = normalize(fetched_f)
    normed_b = (normed_in * gain_in).astype(jnp.bfloat16)
    hidden_pre = jnp.dot(normed_b, weight_in, preferred_element_type=jnp.float32)
    hidden = jax.nn.silu(hidden_pre)
    gate_part = hidden[:, :width]
    value_b = hidden[:, width : 2 * width].astype(jnp.bfloat16)
    query_b = hidden[:, 2 * width : 3 * width].astype(jnp.bfloat16)
    key_b = hidden[:, 3 * width :].astype(jnp.bfloat16)
    pairs = [jnp.concatenate([key_b, value_b], axis=1)]
    queries = [query_b]
    for shift in range(shifts):
        pairs.append(lax.ppermute(pairs[-1], "seq", forward))
        queries.append(lax.ppermute(queries[-1], "seq", backward))
    mixed = None
    for shift in range(shifts + 1):
        operands = [
            before_flags[max(shift - 1, 0)][None],
            query_b,
            (pairs[shift], 0),
            (pairs[shift], 1),
            marked[:, None],
            before[shift][None, :],
        ]
        if shift:
            operands.append(mixed)
        (mixed,) = attention_call(
            functools.partial(forward_kernel, shift == 0, shift > 0), count, width, operands, 1, 6.0
        )
    normed_mid, inverse_mid = normalize(mixed)
    scaled_mid = normed_mid * gain_mid
    gated = (scaled_mid * gate_part).astype(jnp.bfloat16)
    grad_gated = jnp.einsum("te,de->td", upstream, weight_out, preferred_element_type=jnp.float32)
    grad_gate = grad_gated * scaled_mid
    grad_mixed = norm_back(grad_gated * gate_part * gain_mid, normed_mid, inverse_mid).astype(
        jnp.bfloat16
    )
    ups = [grad_mixed]
    for shift in range(shifts):
        ups.append(lax.ppermute(ups[-1], "seq", backward))
    layer = (fetched_f + jnp.dot(gated, weight_out, preferred_element_type=jnp.float32)).astype(
        jnp.bfloat16
    )
    grad_wout = jnp.einsum("td,te->de", gated, upstream, preferred_element_type=jnp.float32)
    operands = [before_flags, query_b, grad_mixed, marked[:, None]]
    for shift in range(shifts + 1):
        operands += [(pairs[shift], 0), (pairs[shift], 1), before[shift][None, :]]
    (grad_query,) = attention_call(
        functools.partial(query_kernel, shifts), count, width, operands, 1, 8.0
    )
    sums = []
    for shift in range(shifts + 1):
        operands = [
            after_flags[max(shift - 1, 0)][None],
            (pairs[0], 0),
            (pairs[0], 1),
            marked[:, None],
            queries[shift],
            ups[shift],
            after[shift][None, :],
        ]
        sums = attention_call(
            functools.partial(key_kernel, shift == 0), count, width, operands + list(sums), 2, 5.0
        )
    grad_key, grad_value = sums
    gate_pre = (grad_gate * silu_slope(hidden_pre[:, :width])).astype(jnp.bfloat16)
    grad_rest = jnp.concatenate([grad_value, grad_query, grad_key], axis=1)
    rest_pre = (grad_rest * silu_slope(hidden_pre[:, width:])).astype(jnp.bfloat16)
    grad_pre = jnp.concatenate([gate_pre, rest_pre], axis=1)
    grad_win = jnp.einsum("td,tf->df", normed_b, grad_pre, preferred_element_type=jnp.float32)
    grad_normed = jnp.einsum("tf,df->td", grad_pre, weight_in, preferred_element_type=jnp.float32)
    grad_rows = norm_back(grad_normed * gain_in, normed_in, inverse_in) + upstream.astype(
        jnp.float32
    )
    outgoing = jnp.dot(in_slot, grad_rows.astype(jnp.bfloat16), preferred_element_type=jnp.float32)
    weight_in_grad, weight_out_grad, incoming = reduce_and_exchange(
        grad_win, grad_wout, outgoing.reshape(devices, capacity, width).astype(jnp.bfloat16), 3
    )
    table_grad = jnp.dot(
        (shard[:, None] == asked[None, :]).astype(jnp.bfloat16),
        incoming.reshape(devices * capacity, width),
        preferred_element_type=jnp.float32,
    )
    return (layer[None], table_grad, weight_in_grad, weight_out_grad)


def solution(mesh):
    in_specs = (
        P(("users", "seq"), None),
        P("users", "seq"),
        P("users", "seq"),
        P(),
        P(),
        P(),
        P(),
        P("users", "seq", None),
    )
    out_specs = (P("users", "seq", None), P(("users", "seq"), None), P(), P())
    return jax.shard_map(body, mesh=mesh, in_specs=in_specs, out_specs=out_specs, check_vma=False)
```

```python
import functools

import jax
import jax.numpy as jnp
from jax import lax
from jax.experimental import pallas as pl
from jax.experimental.pallas import tpu as pltpu
from jax.sharding import PartitionSpec as P

HEADS = 8
HEAD_DIM = 64


epsilon = 1e-05


def normalize(values):
    centred = values - jnp.mean(values, axis=-1, keepdims=True)
    inverse = lax.rsqrt(jnp.mean(centred * centred, axis=-1, keepdims=True) + epsilon)
    return (centred * inverse, inverse)


def norm_back(grad_hat, normed, inverse):
    return inverse * (
        grad_hat
        - jnp.mean(grad_hat, axis=-1, keepdims=True)
        - normed * jnp.mean(grad_hat * normed, axis=-1, keepdims=True)
    )


def silu_slope(values):
    sigma = jax.nn.sigmoid(values)
    return sigma * (1.0 + values * (1.0 - sigma))


PAIR = 2 * HEAD_DIM
SCALE = HEAD_DIM ** (-0.5)


def nt(left, right):
    return lax.dot_general(left, right, (((1,), (1,)), ((), ())), preferred_element_type=jnp.float32)


def silu_parts(scores):
    sigma = 0.5 * jnp.tanh(0.5 * scores) + 0.5
    return sigma, scores * sigma


def visible_of(query_seg, key_seg, rows, columns, row_start, triangular, transposed):
    visible = query_seg == key_seg
    if triangular:
        row = lax.broadcasted_iota(jnp.int32, (rows, columns), 0) + row_start
        column = lax.broadcasted_iota(jnp.int32, (rows, columns), 1)
        visible &= (row <= column) if transposed else (column <= row)
    return visible


def chunk_of(count):
    return 128 if count % 128 == 0 else count


def forward_kernel(triangular, has_acc, flag_ref, q_ref, k_ref, v_ref, segq_ref, segk_ref, *rest):
    acc_ref, out_ref = rest if has_acc else (None, rest[0])
    count = q_ref.shape[0]
    step = chunk_of(count)
    if has_acc:
        out_ref[...] = acc_ref[...]

    def work():
        for start in range(0, count, step):
            rows = slice(start, start + step)
            limit = start + step if triangular else count
            visible = visible_of(
                segq_ref[rows, :], segk_ref[:, :limit], step, limit, start, triangular, False
            )
            parts = []
            for head in range(2):
                lanes = slice(head * HEAD_DIM, (head + 1) * HEAD_DIM)
                scores = nt(q_ref[rows, lanes], k_ref[:limit, lanes]) * SCALE
                _, weights = silu_parts(scores)
                weights = jnp.where(visible, weights, 0.0).astype(jnp.bfloat16)
                parts.append(
                    jnp.dot(weights, v_ref[:limit, lanes], preferred_element_type=jnp.float32)
                )
            both = jnp.concatenate(parts, axis=1)
            if has_acc:
                out_ref[rows, :] += both
            else:
                out_ref[rows, :] = both

    if has_acc:
        pl.when(flag_ref[0] != 0)(work)
    else:
        work()


def query_kernel(shifts, flag_ref, q_ref, up_ref, segq_ref, *rest):
    keys, out_ref = rest[:-1], rest[-1]
    count = q_ref.shape[0]
    step = chunk_of(count)
    for shift in range(shifts + 1):
        k_ref, v_ref, segk_ref = keys[3 * shift : 3 * shift + 3]

        def work(shift=shift, k_ref=k_ref, v_ref=v_ref, segk_ref=segk_ref):
            for start in range(0, count, step):
                rows = slice(start, start + step)
                limit = start + step if shift == 0 else count
                visible = visible_of(
                    segq_ref[rows, :], segk_ref[:, :limit], step, limit, start, shift == 0, False
                )
                parts = []
                for head in range(2):
                    lanes = slice(head * HEAD_DIM, (head + 1) * HEAD_DIM)
                    scores = nt(q_ref[rows, lanes], k_ref[:limit, lanes]) * SCALE
                    sigma, weights = silu_parts(scores)
                    slope = sigma + weights * (1.0 - sigma)
                    dweights = nt(up_ref[rows, lanes], v_ref[:limit, lanes])
                    dscores = jnp.where(visible, dweights * slope, 0.0).astype(jnp.bfloat16)
                    parts.append(
                        jnp.dot(dscores, k_ref[:limit, lanes], preferred_element_type=jnp.float32)
                    )
                both = jnp.concatenate(parts, axis=1) * SCALE
                if shift == 0:
                    out_ref[rows, :] = both
                else:
                    out_ref[rows, :] += both

        if shift == 0:
            work()
        else:
            pl.when(flag_ref[shift - 1] != 0)(work)


def key_kernel(triangular, flag_ref, k_ref, v_ref, segk_ref, q_ref, up_ref, segq_ref, *rest):
    dk_ref, dv_ref = rest[-2:]
    count = k_ref.shape[0]
    step = chunk_of(count)
    if not triangular:
        dk_ref[...] = rest[0][...]
        dv_ref[...] = rest[1][...]

    def work():
        for start in range(0, count, step):
            rows = slice(start, start + step)
            first = start if triangular else 0
            visible = segk_ref[rows, :] == segq_ref[:, first:]
            if triangular:
                row = lax.broadcasted_iota(jnp.int32, (step, count - first), 0)
                column = lax.broadcasted_iota(jnp.int32, (step, count - first), 1)
                visible &= row <= column
            parts_k, parts_v = [], []
            for head in range(2):
                lanes = slice(head * HEAD_DIM, (head + 1) * HEAD_DIM)
                query, up = q_ref[first:, lanes], up_ref[first:, lanes]
                scores = nt(k_ref[rows, lanes], query) * SCALE
                sigma, weights = silu_parts(scores)
                slope = sigma + weights * (1.0 - sigma)
                dweights = nt(v_ref[rows, lanes], up)
                dscores = jnp.where(visible, dweights * slope, 0.0).astype(jnp.bfloat16)
                weights = jnp.where(visible, weights, 0.0).astype(jnp.bfloat16)
                parts_k.append(jnp.dot(dscores, query, preferred_element_type=jnp.float32))
                parts_v.append(jnp.dot(weights, up, preferred_element_type=jnp.float32))
            both_k = jnp.concatenate(parts_k, axis=1) * SCALE
            both_v = jnp.concatenate(parts_v, axis=1)
            if triangular:
                dk_ref[rows, :] = both_k
                dv_ref[rows, :] = both_v
            else:
                dk_ref[rows, :] += both_k
                dv_ref[rows, :] += both_v

    if triangular:
        work()
    else:
        pl.when(flag_ref[0] != 0)(work)


def attention_call(kernel, count, width, operands, results, micros):
    shift_of = lambda offset: (lambda i: (0, i + offset))
    specs, arrays = [], []
    for operand in operands:
        array, offset = operand if isinstance(operand, tuple) else (operand, 0)
        arrays.append(array)
        if array.ndim == 1:
            specs.append(pl.BlockSpec(memory_space=pltpu.SMEM))
        elif array.shape[0] == count and array.shape[1] % width == 0:
            specs.append(pl.BlockSpec((count, PAIR), shift_of(offset * (width // PAIR))))
        else:
            specs.append(pl.BlockSpec(array.shape, lambda i: (0, 0)))
    out = pl.BlockSpec((count, PAIR), lambda i: (0, i))
    shape = jax.ShapeDtypeStruct((count, width), jnp.float32)
    return pl.pallas_call(
        kernel,
        grid=(width // PAIR,),
        in_specs=specs,
        out_specs=[out] * results,
        out_shape=[shape] * results,
        cost_estimate=pl.CostEstimate(
            flops=int(micros * 1.1e9), bytes_accessed=count * width * 2, transcendentals=0
        ),
    )(*arrays)


MESH_ID = pl.DeviceIdType.MESH
LANES = 128


def place(index, ring):
    return (index // ring, lax.rem(index, ring))


def my_index():
    return lax.axis_index("users") * lax.axis_size("seq") + lax.axis_index("seq")


def greet_all(devices, ring):
    barrier = pltpu.get_barrier_semaphore()
    me = my_index()

    def greet(step, carry):
        target = place(lax.rem(me + step, devices), ring)
        pl.semaphore_signal(barrier, inc=1, device_id=target, device_id_type=MESH_ID)
        return carry

    lax.fori_loop(1, devices, greet, 0)
    pl.semaphore_wait(barrier, devices - 1)


def exchange_copy(devices, ring, step, out_ref, in_ref, send_sem, recv_sem):
    me = my_index()
    target = lax.rem(me + step, devices)
    return pltpu.make_async_remote_copy(
        src_ref=out_ref.at[target],
        dst_ref=in_ref.at[me],
        send_sem=send_sem.at[step],
        recv_sem=recv_sem.at[step],
        device_id=place(target, ring),
        device_id_type=MESH_ID,
    )


def exchange_start(devices, ring, out_ref, in_ref, send_sem, recv_sem, first=1, last=None):
    me = my_index()

    def start(step, carry):
        exchange_copy(devices, ring, step, out_ref, in_ref, send_sem, recv_sem).start()
        return carry

    lax.fori_loop(first, devices if last is None else last, start, 0)
    if first == 1:
        pltpu.make_async_copy(out_ref.at[me], in_ref.at[me], send_sem.at[0]).start()


def exchange_wait(devices, ring, out_ref, in_ref, send_sem, recv_sem):
    me = my_index()

    def wait(step, carry):
        exchange_copy(devices, ring, step, out_ref, in_ref, send_sem, recv_sem).wait()
        return carry

    lax.fori_loop(1, devices, wait, 0)
    pltpu.make_async_copy(out_ref.at[me], in_ref.at[me], send_sem.at[0]).wait()


def exchange_kernel(devices, ring, out_ref, in_ref, send_sem, recv_sem):
    greet_all(devices, ring)
    exchange_start(devices, ring, out_ref, in_ref, send_sem, recv_sem)
    exchange_wait(devices, ring, out_ref, in_ref, send_sem, recv_sem)


def exchange(blocks, identity):
    devices, ring = blocks.shape[0], lax.axis_size("seq")
    return pl.pallas_call(
        functools.partial(exchange_kernel, devices, ring),
        out_shape=jax.ShapeDtypeStruct(blocks.shape, blocks.dtype),
        in_specs=[pl.BlockSpec(memory_space=pltpu.VMEM)],
        out_specs=pl.BlockSpec(memory_space=pltpu.VMEM),
        scratch_shapes=[pltpu.SemaphoreType.DMA((devices,)), pltpu.SemaphoreType.DMA((devices,))],
        compiler_params=pltpu.CompilerParams(collective_id=identity, has_side_effects=True),
    )(blocks)


ROWS_UNIT = 16


def bits_of(size):
    return [1 << bit for bit in range(size.bit_length() - 1)]


def orders_of(users, parts):
    bits = bits_of(users)
    turned = bits[:1] + bits[1:][::-1]
    return [bits, turned][:parts]


def chunks(total, start_of, body):
    group = 4 if total % 4 == 0 else total

    def step(index, carry):
        body(index * group, group)
        return carry

    lax.fori_loop(0, total // group, step, 0)


def reduce_kernel(users, ring, parts, pieces, *refs):
    stages = len(bits_of(users))
    win_ref, wout_ref, out_ref, win_out, wout_out, in_ref, acc, gathered = refs[:8]
    rest = list(refs[8:])
    sends = [[rest.pop(0) for _ in range(stages + 1)] for _ in range(parts)]
    recvs = [[rest.pop(0) for _ in range(stages + 1)] for _ in range(parts)]
    a2a_send, a2a_recv, half_send, half_recv, ring_send, ring_recv = rest[:6]
    back_send, back_recv, share_send, share_recv = rest[6:]
    devices = users * ring
    me_u, me_s = lax.axis_index("users"), lax.axis_index("seq")
    units = acc.shape[0]
    span = acc.shape[2]
    win_width = win_ref.shape[1]
    orders = orders_of(users, parts)
    per_part = units // parts

    def packed(block):
        rows = pl.ds(pl.multiple_of(block * ROWS_UNIT, ROWS_UNIT), ROWS_UNIT)
        both = jnp.concatenate([win_ref[rows, :], wout_ref[rows, :]], axis=1)
        return [both[:, piece * span : (piece + 1) * span] for piece in range(pieces)]

    greet_all(devices, ring)

    def bit_at(order, stage):
        return lax.rem(me_u // order[stage], 2)

    def partner_of(order, stage):
        bit = bit_at(order, stage)
        return (me_u + order[stage] - 2 * order[stage] * bit, me_s)

    bases = [part * per_part for part in range(parts)]
    size = per_part
    history = []
    for stage in range(stages):
        half = size // 2
        history.append((list(bases), half))
        copies = []
        for part in range(parts):
            bit = bit_at(orders[part], stage)
            keep, give = bases[part] + bit * half, bases[part] + (1 - bit) * half
            buffer = sends[part][stage]
            if stage == 0:

                def pack_give(index, carry, give=give, buffer=buffer):
                    for piece, value in enumerate(packed(give // pieces + index)):
                        buffer[index * pieces + piece] = value.astype(jnp.bfloat16)
                    return carry

                lax.fori_loop(0, half // pieces, pack_give, 0)
            else:

                def cast_give(first, group, give=give, buffer=buffer):
                    buffer[pl.ds(first, group)] = acc[pl.ds(give + first, group)].astype(jnp.bfloat16)

                chunks(half, 0, cast_give)
            copy = pltpu.make_async_remote_copy(
                src_ref=buffer,
                dst_ref=recvs[part][stage],
                send_sem=half_send.at[part, stage],
                recv_sem=half_recv.at[part, stage],
                device_id=partner_of(orders[part], stage),
                device_id_type=MESH_ID,
            )
            copy.start()
            copies.append(copy)
            bases[part] = keep
        if stage == 0:
            exchange_start(devices, ring, out_ref, in_ref, a2a_send, a2a_recv, 1, devices // 2)
        for part in range(parts):
            keep, buffer = bases[part], recvs[part][stage]
            copies[part].wait()
            if stage == 0:

                def pack_keep(index, carry, keep=keep, buffer=buffer):
                    for piece, value in enumerate(packed(keep // pieces + index)):
                        unit = index * pieces + piece
                        acc[keep + unit] = value + buffer[unit].astype(jnp.float32)
                    return carry

                lax.fori_loop(0, half // pieces, pack_keep, 0)
            else:

                def add_keep(first, group, keep=keep, buffer=buffer):
                    acc[pl.ds(keep + first, group)] += buffer[pl.ds(first, group)].astype(jnp.float32)

                chunks(half, 0, add_keep)
        size = half

    own = size // ring
    copies = []
    for part in range(parts):
        buffer = sends[part][stages]

        def cast_ring(first, group, base=bases[part], buffer=buffer):
            buffer[pl.ds(first, group)] = acc[pl.ds(base + first, group)].astype(jnp.bfloat16)

        chunks(size, 0, cast_ring)
        for step in range(1, ring):
            target = lax.rem(me_s + step, ring)
            copy = pltpu.make_async_remote_copy(
                src_ref=buffer.at[pl.ds(target * own, own)],
                dst_ref=recvs[part][stages].at[step - 1],
                send_sem=ring_send.at[part, step - 1],
                recv_sem=ring_recv.at[part, step - 1],
                device_id=(me_u, target),
                device_id_type=MESH_ID,
            )
            copy.start()
            copies.append(copy)
    for copy in copies:
        copy.wait()
    copies = []
    for part in range(parts):
        mine = bases[part] + me_s * own
        for unit in range(own):
            total = acc[mine + unit]
            for step in range(1, ring):
                total = total + recvs[part][stages][step - 1, unit].astype(jnp.float32)
            gathered[mine + unit] = total.astype(jnp.bfloat16)
        for step in range(1, ring):
            target = lax.rem(me_s + step, ring)
            copy = pltpu.make_async_remote_copy(
                src_ref=gathered.at[pl.ds(mine, own)],
                dst_ref=gathered.at[pl.ds(mine, own)],
                send_sem=share_send.at[part, step - 1],
                recv_sem=share_recv.at[part, step - 1],
                device_id=(me_u, target),
                device_id_type=MESH_ID,
            )
            copy.start()
            copies.append(copy)
    for copy in copies:
        copy.wait()
    for stage in reversed(range(stages)):
        copies = []
        for part in range(parts):
            held = pl.ds(bases[part], size)
            copy = pltpu.make_async_remote_copy(
                src_ref=gathered.at[held],
                dst_ref=gathered.at[held],
                send_sem=back_send.at[part, stage],
                recv_sem=back_recv.at[part, stage],
                device_id=partner_of(orders[part], stage),
                device_id_type=MESH_ID,
            )
            copy.start()
            copies.append(copy)
        if stage == stages - 1:
            exchange_start(devices, ring, out_ref, in_ref, a2a_send, a2a_recv, devices // 2)
        for copy in copies:
            copy.wait()
        bases, size = history[stage][0], size * 2

    def unpack(block, carry):
        rows = pl.ds(pl.multiple_of(block * ROWS_UNIT, ROWS_UNIT), ROWS_UNIT)
        both = jnp.concatenate([gathered[block * pieces + piece] for piece in range(pieces)], axis=1)
        win_out[rows, :] = both[:, :win_width]
        wout_out[rows, :] = both[:, win_width:]
        return carry

    lax.fori_loop(0, units // pieces, unpack, 0)
    exchange_wait(devices, ring, out_ref, in_ref, a2a_send, a2a_recv)


def reduce_and_exchange(grad_win, grad_wout, outgoing, identity):
    users, ring = lax.axis_size("users"), lax.axis_size("seq")
    devices = users * ring
    rows, width = grad_win.shape[0], grad_win.shape[1] + grad_wout.shape[1]
    pieces = 4
    span = width // pieces
    units = rows // ROWS_UNIT * pieces
    parts = 2 if units // 2 % devices == 0 else 1
    stages = len(bits_of(users))
    sizes = [units // parts >> (stage + 1) for stage in range(stages)]
    unit = (ROWS_UNIT, span)
    last = sizes[-1]
    send = [pltpu.VMEM((size, *unit), jnp.bfloat16) for size in sizes + [last]]
    recv = [pltpu.VMEM((size, *unit), jnp.bfloat16) for size in sizes]
    recv.append(pltpu.VMEM((ring - 1, last // ring, *unit), jnp.bfloat16))
    dma = pltpu.SemaphoreType.DMA
    vmem = pl.BlockSpec(memory_space=pltpu.VMEM)
    summed_win, summed_wout, incoming = pl.pallas_call(
        functools.partial(reduce_kernel, users, ring, parts, pieces),
        out_shape=[
            jax.ShapeDtypeStruct(grad_win.shape, jnp.bfloat16),
            jax.ShapeDtypeStruct(grad_wout.shape, jnp.bfloat16),
            jax.ShapeDtypeStruct(outgoing.shape, outgoing.dtype),
        ],
        in_specs=[vmem] * 3,
        out_specs=[vmem] * 3,
        scratch_shapes=[
            pltpu.VMEM((units, *unit), jnp.float32),
            pltpu.VMEM((units, *unit), jnp.bfloat16),
            *(send * parts),
            *(recv * parts),
            dma((devices,)),
            dma((devices,)),
            dma((parts, stages)),
            dma((parts, stages)),
            dma((parts, ring - 1)),
            dma((parts, ring - 1)),
            dma((parts, stages)),
            dma((parts, stages)),
            dma((parts, ring - 1)),
            dma((parts, ring - 1)),
        ],
        compiler_params=pltpu.CompilerParams(
            collective_id=identity, has_side_effects=True, vmem_limit_bytes=48 * 1024 * 1024
        ),
    )(grad_win, grad_wout, outgoing)
    return summed_win.astype(jnp.float32), summed_wout.astype(jnp.float32), incoming


def row_at(table, index):
    return lax.dynamic_slice_in_dim(table, index, 1)[0]


def body(item_table, item_ids, segment_ids, weight_in, weight_out, gain_in, gain_mid, cotangent):
    events = item_ids[0]
    segments = segment_ids[0]
    upstream = cotangent[0]
    ring = lax.axis_size("seq")
    shifts = (ring + 1) // 2
    forward = [(i, i + 1) for i in range(ring - 1)]
    backward = [(i + 1, i) for i in range(ring - 1)]
    marked = segments + 1
    count = events.shape[0]
    shard_rows = item_table.shape[0]
    width = item_table.shape[1]
    devices = lax.axis_size(("users", "seq"))
    capacity = 2 * count // devices
    owner_index = events // shard_rows
    owner_hits = (owner_index[:, None] == jnp.arange(devices, dtype=jnp.int32)[None, :]).astype(
        jnp.int32
    )
    arrival = jnp.sum(jnp.cumsum(owner_hits, axis=0) * owner_hits, axis=1) - 1
    slot_of = owner_index * capacity + arrival
    slots = jnp.arange(devices * capacity, dtype=jnp.int32)
    in_slot = slots[:, None] == slot_of[None, :]
    wanted = jnp.sum(jnp.where(in_slot, (events % shard_rows)[None, :], 0), axis=1)
    in_slot = in_slot.astype(jnp.bfloat16)
    requests = jnp.pad(wanted.reshape(devices, 1, capacity), ((0, 0), (0, 0), (0, LANES - capacity)))
    known = jnp.broadcast_to(marked.reshape(1, count // LANES, LANES), (devices, count // LANES, LANES))
    told = exchange(jnp.concatenate([requests, known], axis=1), 1)
    asked = told[:, 0, :capacity].reshape(-1)
    here = lax.axis_index("seq")
    row = lax.dynamic_slice_in_dim(told[:, 1:], lax.axis_index("users") * ring, ring)
    row = jnp.pad(row.reshape(ring, count), ((shifts, shifts), (0, 0)))
    before = [row_at(row, here + shifts - shift) for shift in range(shifts + 1)]
    after = [row_at(row, here + shifts + shift) for shift in range(shifts + 1)]
    before_flags = jnp.stack([(seg[-1] == marked[0]).astype(jnp.int32) for seg in before[1:]])
    after_flags = jnp.stack([(seg[0] == marked[-1]).astype(jnp.int32) for seg in after[1:]])
    shard = jnp.arange(shard_rows, dtype=jnp.int32)
    served = jnp.dot(
        (asked[:, None] == shard[None, :]).astype(jnp.bfloat16),
        item_table,
        preferred_element_type=jnp.float32,
    ).astype(jnp.bfloat16)
    returned = lax.all_to_all(
        served.reshape(devices, capacity, width),
        ("users", "seq"),
        split_axis=0,
        concat_axis=0,
        tiled=True,
    )
    fetched_f = jnp.dot(
        (slot_of[:, None] == slots[None, :]).astype(jnp.bfloat16),
        returned.reshape(devices * capacity, width),
        preferred_element_type=jnp.float32,
    )
    normed_in, inverse_in = normalize(fetched_f)
    normed_b = (normed_in * gain_in).astype(jnp.bfloat16)
    hidden_pre = jnp.dot(normed_b, weight_in, preferred_element_type=jnp.float32)
    hidden = jax.nn.silu(hidden_pre)
    gate_part = hidden[:, :width]
    value_b = hidden[:, width : 2 * width].astype(jnp.bfloat16)
    query_b = hidden[:, 2 * width : 3 * width].astype(jnp.bfloat16)
    key_b = hidden[:, 3 * width :].astype(jnp.bfloat16)
    pairs = [jnp.concatenate([key_b, value_b], axis=1)]
    queries = [query_b]
    for shift in range(shifts):
        pairs.append(lax.ppermute(pairs[-1], "seq", forward))
        queries.append(lax.ppermute(queries[-1], "seq", backward))
    mixed = None
    for shift in range(shifts + 1):
        operands = [
            before_flags[max(shift - 1, 0)][None],
            query_b,
            (pairs[shift], 0),
            (pairs[shift], 1),
            marked[:, None],
            before[shift][None, :],
        ]
        if shift:
            operands.append(mixed)
        (mixed,) = attention_call(
            functools.partial(forward_kernel, shift == 0, shift > 0), count, width, operands, 1, 6.0
        )
    normed_mid, inverse_mid = normalize(mixed)
    scaled_mid = normed_mid * gain_mid
    gated = (scaled_mid * gate_part).astype(jnp.bfloat16)
    grad_gated = jnp.einsum("te,de->td", upstream, weight_out, preferred_element_type=jnp.float32)
    grad_gate = grad_gated * scaled_mid
    grad_mixed = norm_back(grad_gated * gate_part * gain_mid, normed_mid, inverse_mid).astype(
        jnp.bfloat16
    )
    ups = [grad_mixed, lax.ppermute(grad_mixed, "seq", backward)]
    own_up, ups[1] = lax.optimization_barrier((grad_mixed, ups[1]))
    for shift in range(1, shifts):
        ups.append(lax.ppermute(ups[-1], "seq", backward))
    layer = (fetched_f + jnp.dot(gated, weight_out, preferred_element_type=jnp.float32)).astype(
        jnp.bfloat16
    )
    grad_wout = jnp.einsum("td,te->de", gated, upstream, preferred_element_type=jnp.float32)
    operands = [before_flags, query_b, own_up, marked[:, None]]
    for shift in range(shifts + 1):
        operands += [(pairs[shift], 0), (pairs[shift], 1), before[shift][None, :]]
    (grad_query,) = attention_call(
        functools.partial(query_kernel, shifts), count, width, operands, 1, 8.0
    )
    sums = []
    for shift in range(shifts + 1):
        operands = [
            after_flags[max(shift - 1, 0)][None],
            (pairs[0], 0),
            (pairs[0], 1),
            marked[:, None],
            queries[shift],
            ups[shift],
            after[shift][None, :],
        ]
        sums = attention_call(
            functools.partial(key_kernel, shift == 0), count, width, operands + list(sums), 2, 5.0
        )
    grad_key, grad_value = sums
    gate_pre = (grad_gate * silu_slope(hidden_pre[:, :width])).astype(jnp.bfloat16)
    grad_rest = jnp.concatenate([grad_value, grad_query, grad_key], axis=1)
    rest_pre = (grad_rest * silu_slope(hidden_pre[:, width:])).astype(jnp.bfloat16)
    grad_pre = jnp.concatenate([gate_pre, rest_pre], axis=1)
    grad_win = jnp.einsum("td,tf->df", normed_b, grad_pre, preferred_element_type=jnp.float32)
    grad_normed = jnp.einsum("tf,df->td", grad_pre, weight_in, preferred_element_type=jnp.float32)
    grad_rows = norm_back(grad_normed * gain_in, normed_in, inverse_in) + upstream.astype(
        jnp.float32
    )
    outgoing = jnp.dot(in_slot, grad_rows.astype(jnp.bfloat16), preferred_element_type=jnp.float32)
    weight_in_grad, weight_out_grad, incoming = reduce_and_exchange(
        grad_win, grad_wout, outgoing.reshape(devices, capacity, width).astype(jnp.bfloat16), 3
    )
    table_grad = jnp.dot(
        (shard[:, None] == asked[None, :]).astype(jnp.bfloat16),
        incoming.reshape(devices * capacity, width),
        preferred_element_type=jnp.float32,
    )
    return (layer[None], table_grad, weight_in_grad, weight_out_grad)


def solution(mesh):
    in_specs = (
        P(("users", "seq"), None),
        P("users", "seq"),
        P("users", "seq"),
        P(),
        P(),
        P(),
        P(),
        P("users", "seq", None),
    )
    out_specs = (P("users", "seq", None), P(("users", "seq"), None), P(), P())
    return jax.shard_map(body, mesh=mesh, in_specs=in_specs, out_specs=out_specs, check_vma=False)
```

```python
import functools

import jax
import jax.numpy as jnp
from jax import lax
from jax.experimental import pallas as pl
from jax.experimental.pallas import tpu as pltpu
from jax.sharding import PartitionSpec as P

HEADS = 8
HEAD_DIM = 64


epsilon = 1e-05


def normalize(values):
    centred = values - jnp.mean(values, axis=-1, keepdims=True)
    inverse = lax.rsqrt(jnp.mean(centred * centred, axis=-1, keepdims=True) + epsilon)
    return (centred * inverse, inverse)


def norm_back(grad_hat, normed, inverse):
    return inverse * (
        grad_hat
        - jnp.mean(grad_hat, axis=-1, keepdims=True)
        - normed * jnp.mean(grad_hat * normed, axis=-1, keepdims=True)
    )


def silu_slope(values):
    sigma = jax.nn.sigmoid(values)
    return sigma * (1.0 + values * (1.0 - sigma))


PAIR = 2 * HEAD_DIM
SCALE = HEAD_DIM ** (-0.5)


def nt(left, right):
    return lax.dot_general(left, right, (((1,), (1,)), ((), ())), preferred_element_type=jnp.float32)


def silu_parts(scores):
    sigma = 0.5 * jnp.tanh(0.5 * scores) + 0.5
    return sigma, scores * sigma


def visible_of(query_seg, key_seg, rows, columns, row_start, triangular, transposed):
    visible = query_seg == key_seg
    if triangular:
        row = lax.broadcasted_iota(jnp.int32, (rows, columns), 0) + row_start
        column = lax.broadcasted_iota(jnp.int32, (rows, columns), 1)
        visible &= (row <= column) if transposed else (column <= row)
    return visible


def chunk_of(count):
    return 128 if count % 128 == 0 else count


def forward_kernel(triangular, has_acc, flag_ref, q_ref, k_ref, v_ref, segq_ref, segk_ref, *rest):
    acc_ref, out_ref = rest if has_acc else (None, rest[0])
    count = q_ref.shape[0]
    step = chunk_of(count)
    if has_acc:
        out_ref[...] = acc_ref[...]

    def work():
        for start in range(0, count, step):
            rows = slice(start, start + step)
            limit = start + step if triangular else count
            visible = visible_of(
                segq_ref[rows, :], segk_ref[:, :limit], step, limit, start, triangular, False
            )
            parts = []
            for head in range(2):
                lanes = slice(head * HEAD_DIM, (head + 1) * HEAD_DIM)
                scores = nt(q_ref[rows, lanes], k_ref[:limit, lanes]) * SCALE
                _, weights = silu_parts(scores)
                weights = jnp.where(visible, weights, 0.0).astype(jnp.bfloat16)
                parts.append(
                    jnp.dot(weights, v_ref[:limit, lanes], preferred_element_type=jnp.float32)
                )
            both = jnp.concatenate(parts, axis=1)
            if has_acc:
                out_ref[rows, :] += both
            else:
                out_ref[rows, :] = both

    if has_acc:
        pl.when(flag_ref[0] != 0)(work)
    else:
        work()


def query_kernel(shifts, flag_ref, q_ref, up_ref, segq_ref, *rest):
    keys, out_ref = rest[:-1], rest[-1]
    count = q_ref.shape[0]
    step = chunk_of(count)
    for shift in range(shifts + 1):
        k_ref, v_ref, segk_ref = keys[3 * shift : 3 * shift + 3]

        def work(shift=shift, k_ref=k_ref, v_ref=v_ref, segk_ref=segk_ref):
            for start in range(0, count, step):
                rows = slice(start, start + step)
                limit = start + step if shift == 0 else count
                visible = visible_of(
                    segq_ref[rows, :], segk_ref[:, :limit], step, limit, start, shift == 0, False
                )
                parts = []
                for head in range(2):
                    lanes = slice(head * HEAD_DIM, (head + 1) * HEAD_DIM)
                    scores = nt(q_ref[rows, lanes], k_ref[:limit, lanes]) * SCALE
                    sigma, weights = silu_parts(scores)
                    slope = sigma + weights * (1.0 - sigma)
                    dweights = nt(up_ref[rows, lanes], v_ref[:limit, lanes])
                    dscores = jnp.where(visible, dweights * slope, 0.0).astype(jnp.bfloat16)
                    parts.append(
                        jnp.dot(dscores, k_ref[:limit, lanes], preferred_element_type=jnp.float32)
                    )
                both = jnp.concatenate(parts, axis=1) * SCALE
                if shift == 0:
                    out_ref[rows, :] = both
                else:
                    out_ref[rows, :] += both

        if shift == 0:
            work()
        else:
            pl.when(flag_ref[shift - 1] != 0)(work)


def key_kernel(triangular, flag_ref, k_ref, v_ref, segk_ref, q_ref, up_ref, segq_ref, *rest):
    dk_ref, dv_ref = rest[-2:]
    count = k_ref.shape[0]
    step = chunk_of(count)
    if not triangular:
        dk_ref[...] = rest[0][...]
        dv_ref[...] = rest[1][...]

    def work():
        for start in range(0, count, step):
            rows = slice(start, start + step)
            first = start if triangular else 0
            visible = segk_ref[rows, :] == segq_ref[:, first:]
            if triangular:
                row = lax.broadcasted_iota(jnp.int32, (step, count - first), 0)
                column = lax.broadcasted_iota(jnp.int32, (step, count - first), 1)
                visible &= row <= column
            parts_k, parts_v = [], []
            for head in range(2):
                lanes = slice(head * HEAD_DIM, (head + 1) * HEAD_DIM)
                query, up = q_ref[first:, lanes], up_ref[first:, lanes]
                scores = nt(k_ref[rows, lanes], query) * SCALE
                sigma, weights = silu_parts(scores)
                slope = sigma + weights * (1.0 - sigma)
                dweights = nt(v_ref[rows, lanes], up)
                dscores = jnp.where(visible, dweights * slope, 0.0).astype(jnp.bfloat16)
                weights = jnp.where(visible, weights, 0.0).astype(jnp.bfloat16)
                parts_k.append(jnp.dot(dscores, query, preferred_element_type=jnp.float32))
                parts_v.append(jnp.dot(weights, up, preferred_element_type=jnp.float32))
            both_k = jnp.concatenate(parts_k, axis=1) * SCALE
            both_v = jnp.concatenate(parts_v, axis=1)
            if triangular:
                dk_ref[rows, :] = both_k
                dv_ref[rows, :] = both_v
            else:
                dk_ref[rows, :] += both_k
                dv_ref[rows, :] += both_v

    if triangular:
        work()
    else:
        pl.when(flag_ref[0] != 0)(work)


def attention_call(kernel, count, width, operands, results, micros):
    shift_of = lambda offset: (lambda i: (0, i + offset))
    specs, arrays = [], []
    for operand in operands:
        array, offset = operand if isinstance(operand, tuple) else (operand, 0)
        arrays.append(array)
        if array.ndim == 1:
            specs.append(pl.BlockSpec(memory_space=pltpu.SMEM))
        elif array.shape[0] == count and array.shape[1] % width == 0:
            specs.append(pl.BlockSpec((count, PAIR), shift_of(offset * (width // PAIR))))
        else:
            specs.append(pl.BlockSpec(array.shape, lambda i: (0, 0)))
    out = pl.BlockSpec((count, PAIR), lambda i: (0, i))
    shape = jax.ShapeDtypeStruct((count, width), jnp.float32)
    return pl.pallas_call(
        kernel,
        grid=(width // PAIR,),
        in_specs=specs,
        out_specs=[out] * results,
        out_shape=[shape] * results,
        cost_estimate=pl.CostEstimate(
            flops=int(micros * 1.1e9), bytes_accessed=count * width * 2, transcendentals=0
        ),
    )(*arrays)


MESH_ID = pl.DeviceIdType.MESH
LANES = 128


def place(index, ring):
    return (index // ring, lax.rem(index, ring))


def my_index():
    return lax.axis_index("users") * lax.axis_size("seq") + lax.axis_index("seq")


def greet_all(devices, ring):
    barrier = pltpu.get_barrier_semaphore()
    me = my_index()

    def greet(step, carry):
        target = place(lax.rem(me + step, devices), ring)
        pl.semaphore_signal(barrier, inc=1, device_id=target, device_id_type=MESH_ID)
        return carry

    lax.fori_loop(1, devices, greet, 0)
    pl.semaphore_wait(barrier, devices - 1)


def exchange_copy(devices, ring, step, out_ref, in_ref, send_sem, recv_sem):
    me = my_index()
    target = lax.rem(me + step, devices)
    return pltpu.make_async_remote_copy(
        src_ref=out_ref.at[target],
        dst_ref=in_ref.at[me],
        send_sem=send_sem.at[step],
        recv_sem=recv_sem.at[step],
        device_id=place(target, ring),
        device_id_type=MESH_ID,
    )


def exchange_start(devices, ring, out_ref, in_ref, send_sem, recv_sem):
    me = my_index()

    def start(step, carry):
        exchange_copy(devices, ring, step, out_ref, in_ref, send_sem, recv_sem).start()
        return carry

    lax.fori_loop(1, devices, start, 0)
    pltpu.make_async_copy(out_ref.at[me], in_ref.at[me], send_sem.at[0]).start()


def exchange_wait(devices, ring, out_ref, in_ref, send_sem, recv_sem):
    me = my_index()

    def wait(step, carry):
        exchange_copy(devices, ring, step, out_ref, in_ref, send_sem, recv_sem).wait()
        return carry

    lax.fori_loop(1, devices, wait, 0)
    pltpu.make_async_copy(out_ref.at[me], in_ref.at[me], send_sem.at[0]).wait()


def exchange_kernel(devices, ring, out_ref, in_ref, send_sem, recv_sem):
    greet_all(devices, ring)
    exchange_start(devices, ring, out_ref, in_ref, send_sem, recv_sem)
    exchange_wait(devices, ring, out_ref, in_ref, send_sem, recv_sem)


def exchange(blocks, identity):
    devices, ring = blocks.shape[0], lax.axis_size("seq")
    return pl.pallas_call(
        functools.partial(exchange_kernel, devices, ring),
        out_shape=jax.ShapeDtypeStruct(blocks.shape, blocks.dtype),
        in_specs=[pl.BlockSpec(memory_space=pltpu.VMEM)],
        out_specs=pl.BlockSpec(memory_space=pltpu.VMEM),
        scratch_shapes=[pltpu.SemaphoreType.DMA((devices,)), pltpu.SemaphoreType.DMA((devices,))],
        compiler_params=pltpu.CompilerParams(collective_id=identity, has_side_effects=True),
    )(blocks)


ROWS_UNIT = 16


def bits_of(size):
    return [1 << bit for bit in range(size.bit_length() - 1)]


def orders_of(users, parts):
    bits = bits_of(users)
    turned = bits[:1] + bits[1:][::-1]
    return [bits, turned][:parts]


def chunks(total, start_of, body):
    group = 4 if total % 4 == 0 else total

    def step(index, carry):
        body(index * group, group)
        return carry

    lax.fori_loop(0, total // group, step, 0)


def reduce_kernel(users, ring, parts, pieces, *refs):
    stages = len(bits_of(users))
    win_ref, wout_ref, out_ref, win_out, wout_out, in_ref, acc, gathered = refs[:8]
    rest = list(refs[8:])
    sends = [[rest.pop(0) for _ in range(stages + 1)] for _ in range(parts)]
    recvs = [[rest.pop(0) for _ in range(stages + 1)] for _ in range(parts)]
    a2a_send, a2a_recv, half_send, half_recv, ring_send, ring_recv = rest[:6]
    back_send, back_recv, share_send, share_recv = rest[6:]
    devices = users * ring
    me_u, me_s = lax.axis_index("users"), lax.axis_index("seq")
    units = acc.shape[0]
    span = acc.shape[2]
    win_width = win_ref.shape[1]
    orders = orders_of(users, parts)
    per_part = units // parts

    def packed(block):
        rows = pl.ds(pl.multiple_of(block * ROWS_UNIT, ROWS_UNIT), ROWS_UNIT)
        both = jnp.concatenate([win_ref[rows, :], wout_ref[rows, :]], axis=1)
        return [both[:, piece * span : (piece + 1) * span] for piece in range(pieces)]

    greet_all(devices, ring)
    exchange_start(devices, ring, out_ref, in_ref, a2a_send, a2a_recv)

    def bit_at(order, stage):
        return lax.rem(me_u // order[stage], 2)

    def partner_of(order, stage):
        bit = bit_at(order, stage)
        return (me_u + order[stage] - 2 * order[stage] * bit, me_s)

    bases = [part * per_part for part in range(parts)]
    size = per_part
    history = []
    for stage in range(stages):
        half = size // 2
        history.append((list(bases), half))
        copies = []
        for part in range(parts):
            bit = bit_at(orders[part], stage)
            keep, give = bases[part] + bit * half, bases[part] + (1 - bit) * half
            buffer = sends[part][stage]
            if stage == 0:

                def pack_give(index, carry, give=give, buffer=buffer):
                    for piece, value in enumerate(packed(give // pieces + index)):
                        buffer[index * pieces + piece] = value.astype(jnp.bfloat16)
                    return carry

                lax.fori_loop(0, half // pieces, pack_give, 0)
            else:

                def cast_give(first, group, give=give, buffer=buffer):
                    buffer[pl.ds(first, group)] = acc[pl.ds(give + first, group)].astype(jnp.bfloat16)

                chunks(half, 0, cast_give)
            copy = pltpu.make_async_remote_copy(
                src_ref=buffer,
                dst_ref=recvs[part][stage],
                send_sem=half_send.at[part, stage],
                recv_sem=half_recv.at[part, stage],
                device_id=partner_of(orders[part], stage),
                device_id_type=MESH_ID,
            )
            copy.start()
            copies.append(copy)
            bases[part] = keep
        for part in range(parts):
            keep, buffer = bases[part], recvs[part][stage]
            copies[part].wait()
            if stage == 0:

                def pack_keep(index, carry, keep=keep, buffer=buffer):
                    for piece, value in enumerate(packed(keep // pieces + index)):
                        unit = index * pieces + piece
                        acc[keep + unit] = value + buffer[unit].astype(jnp.float32)
                    return carry

                lax.fori_loop(0, half // pieces, pack_keep, 0)
            else:

                def add_keep(first, group, keep=keep, buffer=buffer):
                    acc[pl.ds(keep + first, group)] += buffer[pl.ds(first, group)].astype(jnp.float32)

                chunks(half, 0, add_keep)
        size = half

    own = size // ring
    copies = []
    for part in range(parts):
        buffer = sends[part][stages]

        def cast_ring(first, group, base=bases[part], buffer=buffer):
            buffer[pl.ds(first, group)] = acc[pl.ds(base + first, group)].astype(jnp.bfloat16)

        chunks(size, 0, cast_ring)
        for step in range(1, ring):
            target = lax.rem(me_s + step, ring)
            copy = pltpu.make_async_remote_copy(
                src_ref=buffer.at[pl.ds(target * own, own)],
                dst_ref=recvs[part][stages].at[step - 1],
                send_sem=ring_send.at[part, step - 1],
                recv_sem=ring_recv.at[part, step - 1],
                device_id=(me_u, target),
                device_id_type=MESH_ID,
            )
            copy.start()
            copies.append(copy)
    for copy in copies:
        copy.wait()
    copies = []
    for part in range(parts):
        mine = bases[part] + me_s * own
        for unit in range(own):
            total = acc[mine + unit]
            for step in range(1, ring):
                total = total + recvs[part][stages][step - 1, unit].astype(jnp.float32)
            gathered[mine + unit] = total.astype(jnp.bfloat16)
        for step in range(1, ring):
            target = lax.rem(me_s + step, ring)
            copy = pltpu.make_async_remote_copy(
                src_ref=gathered.at[pl.ds(mine, own)],
                dst_ref=gathered.at[pl.ds(mine, own)],
                send_sem=share_send.at[part, step - 1],
                recv_sem=share_recv.at[part, step - 1],
                device_id=(me_u, target),
                device_id_type=MESH_ID,
            )
            copy.start()
            copies.append(copy)
    for copy in copies:
        copy.wait()
    for stage in reversed(range(stages)):
        copies = []
        for part in range(parts):
            held = pl.ds(bases[part], size)
            copy = pltpu.make_async_remote_copy(
                src_ref=gathered.at[held],
                dst_ref=gathered.at[held],
                send_sem=back_send.at[part, stage],
                recv_sem=back_recv.at[part, stage],
                device_id=partner_of(orders[part], stage),
                device_id_type=MESH_ID,
            )
            copy.start()
            copies.append(copy)
        for copy in copies:
            copy.wait()
        bases, size = history[stage][0], size * 2

    def unpack(block, carry):
        rows = pl.ds(pl.multiple_of(block * ROWS_UNIT, ROWS_UNIT), ROWS_UNIT)
        both = jnp.concatenate([gathered[block * pieces + piece] for piece in range(pieces)], axis=1)
        win_out[rows, :] = both[:, :win_width]
        wout_out[rows, :] = both[:, win_width:]
        return carry

    lax.fori_loop(0, units // pieces, unpack, 0)
    exchange_wait(devices, ring, out_ref, in_ref, a2a_send, a2a_recv)


def reduce_and_exchange(grad_win, grad_wout, outgoing, identity):
    users, ring = lax.axis_size("users"), lax.axis_size("seq")
    devices = users * ring
    rows, width = grad_win.shape[0], grad_win.shape[1] + grad_wout.shape[1]
    pieces = 4
    span = width // pieces
    units = rows // ROWS_UNIT * pieces
    parts = 2 if units // 2 % devices == 0 else 1
    stages = len(bits_of(users))
    sizes = [units // parts >> (stage + 1) for stage in range(stages)]
    unit = (ROWS_UNIT, span)
    last = sizes[-1]
    send = [pltpu.VMEM((size, *unit), jnp.bfloat16) for size in sizes + [last]]
    recv = [pltpu.VMEM((size, *unit), jnp.bfloat16) for size in sizes]
    recv.append(pltpu.VMEM((ring - 1, last // ring, *unit), jnp.bfloat16))
    dma = pltpu.SemaphoreType.DMA
    vmem = pl.BlockSpec(memory_space=pltpu.VMEM)
    summed_win, summed_wout, incoming = pl.pallas_call(
        functools.partial(reduce_kernel, users, ring, parts, pieces),
        out_shape=[
            jax.ShapeDtypeStruct(grad_win.shape, jnp.bfloat16),
            jax.ShapeDtypeStruct(grad_wout.shape, jnp.bfloat16),
            jax.ShapeDtypeStruct(outgoing.shape, outgoing.dtype),
        ],
        in_specs=[vmem] * 3,
        out_specs=[vmem] * 3,
        scratch_shapes=[
            pltpu.VMEM((units, *unit), jnp.float32),
            pltpu.VMEM((units, *unit), jnp.bfloat16),
            *(send * parts),
            *(recv * parts),
            dma((devices,)),
            dma((devices,)),
            dma((parts, stages)),
            dma((parts, stages)),
            dma((parts, ring - 1)),
            dma((parts, ring - 1)),
            dma((parts, stages)),
            dma((parts, stages)),
            dma((parts, ring - 1)),
            dma((parts, ring - 1)),
        ],
        compiler_params=pltpu.CompilerParams(
            collective_id=identity, has_side_effects=True, vmem_limit_bytes=48 * 1024 * 1024
        ),
    )(grad_win, grad_wout, outgoing)
    return summed_win.astype(jnp.float32), summed_wout.astype(jnp.float32), incoming


def row_at(table, index):
    return lax.dynamic_slice_in_dim(table, index, 1)[0]


def body(item_table, item_ids, segment_ids, weight_in, weight_out, gain_in, gain_mid, cotangent):
    events = item_ids[0]
    segments = segment_ids[0]
    upstream = cotangent[0]
    ring = lax.axis_size("seq")
    shifts = (ring + 1) // 2
    forward = [(i, i + 1) for i in range(ring - 1)]
    backward = [(i + 1, i) for i in range(ring - 1)]
    marked = segments + 1
    count = events.shape[0]
    shard_rows = item_table.shape[0]
    width = item_table.shape[1]
    devices = lax.axis_size(("users", "seq"))
    capacity = 2 * count // devices
    owner_index = events // shard_rows
    owner_hits = (owner_index[:, None] == jnp.arange(devices, dtype=jnp.int32)[None, :]).astype(
        jnp.int32
    )
    arrival = jnp.sum(jnp.cumsum(owner_hits, axis=0) * owner_hits, axis=1) - 1
    slot_of = owner_index * capacity + arrival
    slots = jnp.arange(devices * capacity, dtype=jnp.int32)
    in_slot = slots[:, None] == slot_of[None, :]
    wanted = jnp.sum(jnp.where(in_slot, (events % shard_rows)[None, :], 0), axis=1)
    in_slot = in_slot.astype(jnp.bfloat16)
    requests = jnp.pad(wanted.reshape(devices, 1, capacity), ((0, 0), (0, 0), (0, LANES - capacity)))
    known = jnp.broadcast_to(marked.reshape(1, count // LANES, LANES), (devices, count // LANES, LANES))
    told = exchange(jnp.concatenate([requests, known], axis=1), 1)
    asked = told[:, 0, :capacity].reshape(-1)
    here = lax.axis_index("seq")
    row = lax.dynamic_slice_in_dim(told[:, 1:], lax.axis_index("users") * ring, ring)
    row = jnp.pad(row.reshape(ring, count), ((shifts, shifts), (0, 0)))
    before = [row_at(row, here + shifts - shift) for shift in range(shifts + 1)]
    after = [row_at(row, here + shifts + shift) for shift in range(shifts + 1)]
    before_flags = jnp.stack([(seg[-1] == marked[0]).astype(jnp.int32) for seg in before[1:]])
    after_flags = jnp.stack([(seg[0] == marked[-1]).astype(jnp.int32) for seg in after[1:]])
    shard = jnp.arange(shard_rows, dtype=jnp.int32)
    served = jnp.dot(
        (asked[:, None] == shard[None, :]).astype(jnp.bfloat16),
        item_table,
        preferred_element_type=jnp.float32,
    ).astype(jnp.bfloat16)
    returned = lax.all_to_all(
        served.reshape(devices, capacity, width),
        ("users", "seq"),
        split_axis=0,
        concat_axis=0,
        tiled=True,
    )
    fetched_f = jnp.dot(
        (slot_of[:, None] == slots[None, :]).astype(jnp.bfloat16),
        returned.reshape(devices * capacity, width),
        preferred_element_type=jnp.float32,
    )
    normed_in, inverse_in = normalize(fetched_f)
    normed_b = (normed_in * gain_in).astype(jnp.bfloat16)
    hidden_pre = jnp.dot(normed_b, weight_in, preferred_element_type=jnp.float32)
    hidden = jax.nn.silu(hidden_pre)
    gate_part = hidden[:, :width]
    value_b = hidden[:, width : 2 * width].astype(jnp.bfloat16)
    query_b = hidden[:, 2 * width : 3 * width].astype(jnp.bfloat16)
    key_b = hidden[:, 3 * width :].astype(jnp.bfloat16)
    pairs = [jnp.concatenate([key_b, value_b], axis=1)]
    queries = [query_b]
    for shift in range(shifts):
        pairs.append(lax.ppermute(pairs[-1], "seq", forward))
        queries.append(lax.ppermute(queries[-1], "seq", backward))
    mixed = None
    for shift in range(shifts + 1):
        operands = [
            before_flags[max(shift - 1, 0)][None],
            query_b,
            (pairs[shift], 0),
            (pairs[shift], 1),
            marked[:, None],
            before[shift][None, :],
        ]
        if shift:
            operands.append(mixed)
        (mixed,) = attention_call(
            functools.partial(forward_kernel, shift == 0, shift > 0), count, width, operands, 1, 6.0
        )
    normed_mid, inverse_mid = normalize(mixed)
    scaled_mid = normed_mid * gain_mid
    gated = (scaled_mid * gate_part).astype(jnp.bfloat16)
    grad_gated = jnp.einsum("te,de->td", upstream, weight_out, preferred_element_type=jnp.float32)
    grad_gate = grad_gated * scaled_mid
    grad_mixed = norm_back(grad_gated * gate_part * gain_mid, normed_mid, inverse_mid).astype(
        jnp.bfloat16
    )
    ups = [grad_mixed, lax.ppermute(grad_mixed, "seq", backward)]
    own_up, ups[1] = lax.optimization_barrier((grad_mixed, ups[1]))
    for shift in range(1, shifts):
        ups.append(lax.ppermute(ups[-1], "seq", backward))
    layer = (fetched_f + jnp.dot(gated, weight_out, preferred_element_type=jnp.float32)).astype(
        jnp.bfloat16
    )
    grad_wout = jnp.einsum("td,te->de", gated, upstream, preferred_element_type=jnp.float32)
    operands = [before_flags, query_b, own_up, marked[:, None]]
    for shift in range(shifts + 1):
        operands += [(pairs[shift], 0), (pairs[shift], 1), before[shift][None, :]]
    (grad_query,) = attention_call(
        functools.partial(query_kernel, shifts), count, width, operands, 1, 8.0
    )
    sums = []
    for shift in range(shifts + 1):
        operands = [
            after_flags[max(shift - 1, 0)][None],
            (pairs[0], 0),
            (pairs[0], 1),
            marked[:, None],
            queries[shift],
            ups[shift],
            after[shift][None, :],
        ]
        sums = attention_call(
            functools.partial(key_kernel, shift == 0), count, width, operands + list(sums), 2, 5.0
        )
    grad_key, grad_value = sums
    gate_pre = (grad_gate * silu_slope(hidden_pre[:, :width])).astype(jnp.bfloat16)
    grad_rest = jnp.concatenate([grad_value, grad_query, grad_key], axis=1)
    rest_pre = (grad_rest * silu_slope(hidden_pre[:, width:])).astype(jnp.bfloat16)
    grad_pre = jnp.concatenate([gate_pre, rest_pre], axis=1)
    grad_win = jnp.einsum("td,tf->df", normed_b, grad_pre, preferred_element_type=jnp.float32)
    grad_normed = jnp.einsum("tf,df->td", grad_pre, weight_in, preferred_element_type=jnp.float32)
    grad_rows = norm_back(grad_normed * gain_in, normed_in, inverse_in) + upstream.astype(
        jnp.float32
    )
    outgoing = jnp.dot(in_slot, grad_rows.astype(jnp.bfloat16), preferred_element_type=jnp.float32)
    weight_in_grad, weight_out_grad, incoming = reduce_and_exchange(
        grad_win, grad_wout, outgoing.reshape(devices, capacity, width).astype(jnp.bfloat16), 3
    )
    table_grad = jnp.dot(
        (shard[:, None] == asked[None, :]).astype(jnp.bfloat16),
        incoming.reshape(devices * capacity, width),
        preferred_element_type=jnp.float32,
    )
    return (layer[None], table_grad, weight_in_grad, weight_out_grad)


def solution(mesh):
    in_specs = (
        P(("users", "seq"), None),
        P("users", "seq"),
        P("users", "seq"),
        P(),
        P(),
        P(),
        P(),
        P("users", "seq", None),
    )
    out_specs = (P("users", "seq", None), P(("users", "seq"), None), P(), P())
    return jax.shard_map(body, mesh=mesh, in_specs=in_specs, out_specs=out_specs, check_vma=False)
```
